256 devices in a mesh: mode: 64 (over y, x_lo, z), pencil: 4 (over x_hi, core).
Axes of the slice: x: 4 (x_hi: 2, x_lo: 2; x = x_hi * 2 + x_lo), y: 4, z: 8, core: 2. Of those that a mesh axis runs over, the one named last changes fastest.
Arguments:
- cotangent: bfloat16 [256, 8, 256, 512], P('mode', None, 'pencil'), may hold values from -6 to 6
- radial_ops: bfloat16 [256, 256, 256], P('mode'), may hold values from -0.375 to 0.375
- lengths: int32 [256], P('mode'), may hold values from 64 to 256, as said below
- couple_one: float32 [8, 8], replicated, may hold values from -1.5 to 1.5
- couple_two: float32 [8, 8], replicated, may hold values from -1.5 to 1.5
- axial_damping: float32 [256, 512], P('mode'), may hold values from 0.2 to 1
Outputs:
- sensitivity: bfloat16 [256, 8, 256, 512], P('mode', None, None, 'pencil')
The draws below stay inside these ranges and needn't reach their ends.
Inputs may be any that keep to these rules, and one draw needn't show every extreme that they name: Mode m keeps its first lengths[m] radial coefficients; mode 0 keeps all 256 and mode 256 / 2 keeps 256 / 4.
All inputs are finite; a program needn't handle non-finite values.
Results may differ from the reference program's by a relative error of at most 0.01.
Values may be sent and summed in bfloat16 or wider, within the bound.
No kernel may reach another device: no remote copies, remote signals or barrier semaphores. Data moves between devices by JAX's collectives and lax.ppermute only.
A program may use at most 128 MiB of HBM per device.

```python
import math
import jax
import jax.numpy as jnp
from jax import lax

NR = 256
NZ = 512
COMP = 8
MODES = 256


def draw_lengths(key, part):
    modes = jnp.arange(MODES, dtype=jnp.int32)
    beside_all = jnp.minimum(modes, MODES - modes)
    base = NR - 3 * NR // 4 * beside_all // (MODES // 2)
    jitter = jax.random.randint(jax.random.fold_in(key, 7), (MODES,), -(NR // 16), NR // 16 + 1, dtype=jnp.int32)
    result = jnp.clip(base + jitter, NR // 4, NR)
    result = result.at[0].set(NR)
    result = result.at[MODES // 2].set(NR // 4)
    return result.astype(jnp.int32)


def levels(rng, dims, pieces, least, largest):
    loudness, own = 1.0, jax.random.fold_in(rng, 6)
    for dim, shards_of in pieces:
        heights = jnp.exp(jax.random.uniform(jax.random.fold_in(own, dim), (shards_of,), jnp.float32, least / len(pieces), largest / len(pieces)))
        loudness = loudness * jnp.repeat(heights, dims[dim] // shards_of).reshape([-1 if axis == dim else 1 for axis in range(len(dims))])
    return loudness


def gaussian(key, extent, scale, bound, split=(), held_as=jnp.bfloat16):
    array = scale * jax.random.normal(key, extent, jnp.float32)
    if split:
        array = array * levels(key, extent, split, -0.22, 0.18)
    return jnp.clip(array, -bound, bound).astype(held_as)


def setup_inputs(seed: int = 0) -> dict:
    keys = jax.random.split(jax.random.key(seed), 7)
    return {
        "cotangent": gaussian(keys[0], (MODES, COMP, NR, NZ), 1.0, 6.0, ((0, 64), (2, 4))),
        "radial_ops": gaussian(keys[1], (MODES, NR, NR), NR ** -0.5, 0.375, ((0, 64),)),
        "lengths": draw_lengths(jax.random.fold_in(keys[6], 71), 0),
        "couple_one": gaussian(keys[3], (COMP, COMP), 16 ** -0.5, 1.5, (), jnp.float32),
        "couple_two": gaussian(keys[4], (COMP, COMP), 16 ** -0.5, 1.5, (), jnp.float32),
        "axial_damping": jnp.clip(jnp.exp(math.log(1.0) - 1.609438 * jax.random.uniform(keys[5], (MODES, NZ), jnp.float32) ** levels(keys[5], (MODES, NZ), ((0, 64),), -0.2, 0.2)), 0.2, 1.0),
    }


HIGH = lax.Precision.HIGHEST

def cosine_table(count):
    points = jnp.arange(count, dtype=jnp.float32)
    scale = jnp.where(points == 0.0, math.sqrt(1.0 / count), math.sqrt(2.0 / count))
    table = jnp.cos(math.pi * (points[:, None] + 0.5) * points[None, :] / count) * scale[None, :]
    return table.astype(jnp.bfloat16)

def couple_modes(field, couple_one, couple_two):

    def single(position):

        def pick(offset):
            return lax.dynamic_index_in_dim(field, (position + offset) % MODES, 0, keepdims=False).astype(jnp.float32)
        near_one = pick(-1) + pick(1)
        near_two = pick(-2) + pick(2)
        mixed = pick(0) + jnp.einsum('dc,drz->crz', couple_one, near_one, precision=HIGH)
        mixed = mixed + jnp.einsum('dc,drz->crz', couple_two, near_two, precision=HIGH)
        return mixed.astype(jnp.bfloat16)
    return lax.map(single, jnp.arange(MODES, dtype=jnp.int32))

def axial_step(field, damping, table):
    tab32 = table.astype(jnp.float32)

    def single(couple):
        sheet, factor = couple
        spectral = jnp.einsum('crz,zk->crk', sheet.astype(jnp.float32), tab32, precision=HIGH) * factor[None, None, :]
        back = jnp.einsum('crk,zk->crz', spectral, tab32, precision=HIGH)
        return back.astype(jnp.bfloat16)
    return lax.map(single, (field, damping))

def radial_step(field, radial_ops, lengths):
    rows = jnp.arange(NR, dtype=jnp.int32)

    def single(triple):
        sheet, matrix, length = triple
        masked = jnp.where((rows < length)[:, None], matrix.astype(jnp.float32), jnp.float32(0.0))
        out = jnp.einsum('rs,crz->csz', masked, sheet.astype(jnp.float32), precision=HIGH)
        return out.astype(jnp.bfloat16)
    return lax.map(single, (field, radial_ops, lengths))

def reference(cotangent, radial_ops, lengths, couple_one, couple_two, axial_damping):
    table = cosine_table(NZ)
    field = cotangent
    for step in range(2):
        field = couple_modes(field, couple_one, couple_two)
        field = axial_step(field, axial_damping, table)
        field = radial_step(field, radial_ops, lengths)
    return field
```

```python
import functools
import math

import jax
import jax.numpy as jnp
import numpy as np
from jax import lax
from jax.experimental import pallas as pl
from jax.experimental.pallas import tpu as pltpu
from jax.sharding import PartitionSpec as P

BF = jnp.bfloat16
F32 = jnp.float32
SUB = 16
VMEM_LIMIT = 48 * 1024 * 1024


def cosine_table(count):
    points = np.arange(count, dtype=np.float32)
    scale = np.where(points == 0.0, np.float32(math.sqrt(1.0 / count)), np.float32(math.sqrt(2.0 / count)))
    angle = np.float32(math.pi) * (points[:, None] + np.float32(0.5)) * points[None, :] / np.float32(count)
    return (np.cos(angle).astype(np.float32) * scale[None, :].astype(np.float32)).astype(BF)


def vmem(count):
    return [pl.BlockSpec(memory_space=pltpu.VMEM)] * count


def call(kernel, name, args, outs, flops, scratch=(), smem=0):
    moved = sum(a.size * a.dtype.itemsize for a in args)
    moved += sum(math.prod(o.shape) * o.dtype.itemsize for o in outs)
    return pl.pallas_call(
        kernel,
        out_shape=outs,
        in_specs=[pl.BlockSpec(memory_space=pltpu.SMEM)] * smem + vmem(len(args) - smem),
        out_specs=vmem(len(outs)),
        scratch_shapes=list(scratch),
        compiler_params=pltpu.CompilerParams(vmem_limit_bytes=VMEM_LIMIT),
        cost_estimate=pl.CostEstimate(flops=flops, bytes_accessed=moved, transcendentals=0),
        name=name,
    )(*args)


def dot(a, b):
    return jnp.dot(a, b, preferred_element_type=F32)


def dot_nt(a, b):
    return lax.dot_general(a, b, (((1,), (1,)), ((), ())), preferred_element_type=F32)


def shape(*dims, dtype=BF):
    return jax.ShapeDtypeStruct(dims, dtype)


def prep_kernel(peers, me_ref, len_ref, q_ref, damp_ref, rad_ref, one_ref, two_ref, m1_ref, mpp_ref, rpp_ref, rp_ref, w_ref, qp_ref):
    me = me_ref[0]
    nz = q_ref.shape[0]
    block = nz // peers
    for k in range(peers):
        start = pl.multiple_of((me ^ k) * block, block)
        qp_ref[k * block : (k + 1) * block, :] = q_ref[pl.ds(start, block), :]
    qp = qp_ref[...]
    for m in range(damp_ref.shape[0]):
        factor = damp_ref[m : m + 1, :]
        for table, out in ((q_ref, m1_ref), (qp_ref, mpp_ref)):
            scaled = table[...].astype(F32) * factor
            high = scaled.astype(BF)
            low = (scaled - high.astype(F32)).astype(BF)
            out[m] = (dot_nt(high, qp) + dot_nt(low, qp)).astype(BF)
    nr = rad_ref.shape[1]
    rows = nr // peers
    for m in range(rad_ref.shape[0]):
        parts = []
        for k in range(peers):
            start = pl.multiple_of((me ^ k) * rows, rows)
            part = rad_ref[m, pl.ds(start, rows), :].astype(F32)
            index = start + lax.broadcasted_iota(jnp.int32, (rows, nr), 0)
            parts.append(jnp.where(index < len_ref[m], part, 0.0))
        turned = jnp.concatenate(parts, axis=0).T.astype(BF)
        rp_ref[m] = turned
        for k in range(peers):
            start = pl.multiple_of((me ^ k) * rows, rows)
            rpp_ref[m, k * rows : (k + 1) * rows, :] = rp_ref[m, pl.ds(start, rows), :]
    comp = one_ref.shape[0]
    wide = comp * SUB
    row = lax.broadcasted_iota(jnp.int32, (wide, comp), 0) // SUB
    spread = jnp.where(row == lax.broadcasted_iota(jnp.int32, (wide, comp), 1), 1.0, 0.0).astype(BF)
    i = lax.broadcasted_iota(jnp.int32, (wide, wide), 0) % SUB
    j = lax.broadcasted_iota(jnp.int32, (wide, wide), 1) % SUB
    for at, ref in enumerate((one_ref, two_ref)):
        turned = ref[...].astype(BF).astype(F32)
        half = lax.dot_general(spread, turned.astype(BF), (((1,), (1,)), ((), ())), preferred_element_type=F32)
        full = dot_nt(half.astype(BF), spread)
        full = jnp.where(i == j, full, 0.0).astype(BF)
        w_ref[:, (2 * at) * wide : (2 * at + 1) * wide] = full
        w_ref[:, (2 * at + 1) * wide : (2 * at + 2) * wide] = full


def prepare(peers, me, lengths, table, damping, radial, one, two):
    modes, nz = damping.shape
    nr = radial.shape[1]
    wide = one.shape[0] * SUB
    return call(
        functools.partial(prep_kernel, peers),
        "prepare",
        (me, lengths, table, damping, radial, one, two),
        [
            shape(modes, nz, nz),
            shape(modes, nz, nz),
            shape(modes, nr, nr),
            shape(modes, nr, nr),
            shape(wide, 4 * wide),
        ],
        8 * modes * nz**3,
        scratch=[pltpu.VMEM((nz, nz), BF)],
        smem=2,
    )


def around(own, before, after, m):
    count = len(own)

    def at(i):
        if i < 0:
            return before[-1 - i]
        return own[i] if i < count else after[i - count]

    return [at(m - 1), at(m + 1), at(m - 2), at(m + 2)]


def couple_axial_kernel(peers, modes, count, *refs):
    x_ref = refs[0]
    before, after = refs[1:3], refs[3:5]
    w_ref, m_ref = refs[5:7]
    outs, a_ref = refs[7 : 7 + peers], refs[7 + peers]
    own = [x_ref.at[i] for i in range(count)]
    comp, rows, nz = own[0].shape
    wide = comp * SUB
    block = nz // peers
    for at, m in enumerate(modes):
        near = around(own, before, after, m)
        for b in range(rows // SUB):
            part = slice(b * SUB, (b + 1) * SUB)
            field = jnp.concatenate([ref[:, part, :].reshape(wide, nz) for ref in near], axis=0)
            mixed = dot(w_ref[...], field) + own[m][:, part, :].reshape(wide, nz).astype(F32)
            a_ref[b * wide : (b + 1) * wide, :] = mixed.astype(BF)
        result = dot(a_ref[...], m_ref[m]).astype(BF)
        for b in range(rows // SUB):
            for k in range(peers):
                piece = result[b * wide : (b + 1) * wide, k * block : (k + 1) * block]
                outs[k][at, :, b * SUB : (b + 1) * SUB, :] = piece.reshape(comp, SUB, block)


def couple_axial(peers, modes, x, before, after, weights, matrices):
    count, comp, rows, nz = x.shape
    return call(
        functools.partial(couple_axial_kernel, peers, modes, count),
        "couple_axial",
        (x, *before, *after, weights, matrices),
        [shape(len(modes), comp, rows, nz // peers)] * peers,
        len(modes) * comp * rows * nz * 2 * (nz + 4 * comp * SUB),
        scratch=[pltpu.VMEM((comp * rows, nz), BF)],
    )


def radial_kernel(peers, modes, *refs):
    pieces, r_ref, outs = refs[:peers], refs[peers], refs[peers + 1 :]
    comp = pieces[0].shape[1]
    block = pieces[0].shape[3]
    for at, m in enumerate(modes):
        matrix = r_ref[m]
        for c in range(0, comp, 2):
            field = jnp.concatenate(
                [jnp.concatenate([p[at, c], p[at, c + 1]], axis=1) for p in pieces], axis=0
            )
            result = dot(matrix, field).astype(BF)
            out = outs[at] if len(outs) > 1 else outs[0].at[at]
            out[c] = result[:, :block]
            out[c + 1] = result[:, block:]


def radial(peers, modes, pieces, matrices, separate):
    count, comp, rows, block = pieces[0].shape
    nr = rows * peers
    outs = [shape(comp, nr, block)] * count if separate else [shape(count, comp, nr, block)]
    return call(
        functools.partial(radial_kernel, peers, modes),
        "radial",
        (*pieces, matrices),
        outs,
        count * comp * nr * nr * block * 2,
    )


def couple_kernel(peers, modes, count, *refs):
    own, before, after = refs[:count], refs[count : count + 2], refs[count + 2 : count + 4]
    w_ref = refs[count + 4]
    outs = refs[count + 5 :]
    comp, nr, block = own[0].shape
    rows = nr // peers
    wide = comp * SUB
    for at, m in enumerate(modes):
        near = around(own, before, after, m)

        def side(ref, k):
            parts = [
                ref[:, k * rows + b * SUB : k * rows + (b + 1) * SUB, :].reshape(wide, block)
                for b in range(rows // SUB)
            ]
            return jnp.concatenate(parts, axis=1)

        for k in range(peers):
            field = jnp.concatenate([side(ref, k) for ref in near], axis=0)
            mixed = (dot(w_ref[...], field) + side(own[m], k).astype(F32)).astype(BF)
            for b in range(rows // SUB):
                piece = mixed[:, b * block : (b + 1) * block]
                outs[k][at, :, b * SUB : (b + 1) * SUB, :] = piece.reshape(comp, SUB, block)


def couple(peers, modes, own, before, after, weights):
    comp, nr, block = own[0].shape
    return call(
        functools.partial(couple_kernel, peers, modes, len(own)),
        "couple",
        (*own, *before, *after, weights),
        [shape(len(modes), comp, nr // peers, block)] * peers,
        len(modes) * comp * nr * block * 2 * 4 * comp * SUB,
    )


def axial_kernel(peers, modes, *refs):
    pieces, m_ref, outs = refs[:peers], refs[peers], refs[peers + 1 :]
    comp, rows, block = pieces[0].shape[1:]
    for at, m in enumerate(modes):
        field = jnp.concatenate([p[at].reshape(comp * rows, block) for p in pieces], axis=1)
        result = dot(field, m_ref[m]).astype(BF)
        for k in range(peers):
            outs[k][at] = result[:, k * block : (k + 1) * block].reshape(comp, rows, block)


def axial(peers, modes, pieces, matrices):
    count, comp, rows, block = pieces[0].shape
    nz = block * peers
    return call(
        functools.partial(axial_kernel, peers, modes),
        "axial",
        (*pieces, matrices),
        [shape(count, comp, rows, block)] * peers,
        count * comp * rows * nz * nz * 2,
    )


def swap(pieces):
    peers = len(pieces)
    result = list(pieces)
    for k in sorted(range(1, peers), key=lambda k: k == 1):
        result[k] = lax.ppermute(pieces[k], "pencil", [(i, i ^ k) for i in range(peers)])
    return result


def local(cotangent, radial_ops, lengths, couple_one, couple_two, axial_damping):
    peers, ring = lax.axis_size("pencil"), lax.axis_size("mode")
    up = [(i, (i + 1) % ring) for i in range(ring)]
    down = [(j, i) for i, j in up]
    count = cotangent.shape[0]
    modes = tuple(range(count))

    def halos(planes):
        before = [lax.ppermute(planes[count - 1 - i], "mode", up) for i in range(2)]
        after = [lax.ppermute(planes[i], "mode", down) for i in range(2)]
        return before, after

    table = jnp.asarray(cosine_table(axial_damping.shape[1]))
    me = lax.axis_index("pencil").astype(jnp.int32).reshape(1)
    before, after = halos([cotangent[i] for i in modes])
    m1, mpp, rpp, rp, weights = prepare(
        peers, me, lengths, table, axial_damping, radial_ops, couple_one, couple_two
    )
    pieces = swap(couple_axial(peers, modes, cotangent, before, after, weights, m1))
    planes = radial(peers, modes, pieces, rpp, True)
    before, after = halos(planes)
    pieces = swap(couple(peers, modes, planes, before, after, weights))
    pieces = swap(axial(peers, modes, pieces, mpp))
    return radial(peers, modes, pieces, rp, False)[0]


def solution(mesh):
    return jax.shard_map(
        local,
        mesh=mesh,
        in_specs=(
            P("mode", None, "pencil", None),
            P("mode", None, None),
            P("mode"),
            P(),
            P(),
            P("mode", None),
        ),
        out_specs=P("mode", None, None, "pencil"),
        check_vma=False,
    )
```

```python
import functools
import math

import jax
import jax.numpy as jnp
import numpy as np
from jax import lax
from jax.experimental import pallas as pl
from jax.experimental.pallas import tpu as pltpu
from jax.sharding import PartitionSpec as P

BF = jnp.bfloat16
F32 = jnp.float32
SUB = 16
VMEM_LIMIT = 48 * 1024 * 1024


def cosine_table(count):
    points = np.arange(count, dtype=np.float32)
    scale = np.where(points == 0.0, np.float32(math.sqrt(1.0 / count)), np.float32(math.sqrt(2.0 / count)))
    angle = np.float32(math.pi) * (points[:, None] + np.float32(0.5)) * points[None, :] / np.float32(count)
    return (np.cos(angle).astype(np.float32) * scale[None, :].astype(np.float32)).astype(BF)


def vmem(count):
    return [pl.BlockSpec(memory_space=pltpu.VMEM)] * count


def call(kernel, name, args, outs, flops, scratch=(), smem=0):
    moved = sum(a.size * a.dtype.itemsize for a in args)
    moved += sum(math.prod(o.shape) * o.dtype.itemsize for o in outs)
    return pl.pallas_call(
        kernel,
        out_shape=outs,
        in_specs=[pl.BlockSpec(memory_space=pltpu.SMEM)] * smem + vmem(len(args) - smem),
        out_specs=vmem(len(outs)),
        scratch_shapes=list(scratch),
        compiler_params=pltpu.CompilerParams(vmem_limit_bytes=VMEM_LIMIT),
        cost_estimate=pl.CostEstimate(flops=flops, bytes_accessed=moved, transcendentals=0),
        name=name,
    )(*args)


def dot(a, b):
    return jnp.dot(a, b, preferred_element_type=F32)


def dot_nt(a, b):
    return lax.dot_general(a, b, (((1,), (1,)), ((), ())), preferred_element_type=F32)


def shape(*dims, dtype=BF):
    return jax.ShapeDtypeStruct(dims, dtype)


def prep_kernel(peers, me_ref, len_ref, q_ref, damp_ref, rad_ref, one_ref, two_ref, m1_ref, mpp_ref, rpp_ref, rp_ref, w_ref, qp_ref):
    me = me_ref[0]
    nz = q_ref.shape[0]
    block = nz // peers
    for k in range(peers):
        start = pl.multiple_of((me ^ k) * block, block)
        qp_ref[k * block : (k + 1) * block, :] = q_ref[pl.ds(start, block), :]
    qp = qp_ref[...]
    for m in range(damp_ref.shape[0]):
        factor = damp_ref[m : m + 1, :]
        for table, out in ((q_ref, m1_ref), (qp_ref, mpp_ref)):
            scaled = table[...].astype(F32) * factor
            high = scaled.astype(BF)
            low = (scaled - high.astype(F32)).astype(BF)
            out[m] = (dot_nt(high, qp) + dot_nt(low, qp)).astype(BF)
    nr = rad_ref.shape[1]
    rows = nr // peers
    for m in range(rad_ref.shape[0]):
        parts = []
        for k in range(peers):
            start = pl.multiple_of((me ^ k) * rows, rows)
            part = rad_ref[m, pl.ds(start, rows), :].astype(F32)
            index = start + lax.broadcasted_iota(jnp.int32, (rows, nr), 0)
            parts.append(jnp.where(index < len_ref[m], part, 0.0))
        turned = jnp.concatenate(parts, axis=0).T.astype(BF)
        rp_ref[m] = turned
        for k in range(peers):
            start = pl.multiple_of((me ^ k) * rows, rows)
            rpp_ref[m, k * rows : (k + 1) * rows, :] = rp_ref[m, pl.ds(start, rows), :]
    comp = one_ref.shape[0]
    wide = comp * SUB
    row = lax.broadcasted_iota(jnp.int32, (wide, comp), 0) // SUB
    spread = jnp.where(row == lax.broadcasted_iota(jnp.int32, (wide, comp), 1), 1.0, 0.0).astype(BF)
    i = lax.broadcasted_iota(jnp.int32, (wide, wide), 0) % SUB
    j = lax.broadcasted_iota(jnp.int32, (wide, wide), 1) % SUB
    for at, ref in enumerate((one_ref, two_ref)):
        turned = ref[...].astype(BF).astype(F32)
        half = lax.dot_general(spread, turned.astype(BF), (((1,), (1,)), ((), ())), preferred_element_type=F32)
        full = dot_nt(half.astype(BF), spread)
        full = jnp.where(i == j, full, 0.0).astype(BF)
        w_ref[:, (2 * at) * wide : (2 * at + 1) * wide] = full
        w_ref[:, (2 * at + 1) * wide : (2 * at + 2) * wide] = full


def prepare(peers, me, lengths, table, damping, radial, one, two):
    modes, nz = damping.shape
    nr = radial.shape[1]
    wide = one.shape[0] * SUB
    return call(
        functools.partial(prep_kernel, peers),
        "prepare",
        (me, lengths, table, damping, radial, one, two),
        [
            shape(modes, nz, nz),
            shape(modes, nz, nz),
            shape(modes, nr, nr),
            shape(modes, nr, nr),
            shape(wide, 4 * wide),
        ],
        8 * modes * nz**3,
        scratch=[pltpu.VMEM((nz, nz), BF)],
        smem=2,
    )


def around(own, before, after, m):
    count = len(own)

    def at(i):
        if i < 0:
            return before[-1 - i]
        return own[i] if i < count else after[i - count]

    return [at(m - 1), at(m + 1), at(m - 2), at(m + 2)]


def couple_axial_kernel(peers, modes, count, depth, *refs):
    x_ref, refs = refs[0], refs[1:]
    before, after, refs = refs[:depth], refs[depth : 2 * depth], refs[2 * depth :]
    w_ref, m_ref = refs[:2]
    outs, a_ref = refs[2 : 2 + peers], refs[2 + peers]
    own = [x_ref.at[i] for i in range(count)]
    comp, rows, nz = own[0].shape
    wide = comp * SUB
    block = nz // peers
    for at, m in enumerate(modes):
        near = around(own, before, after, m)
        for b in range(rows // SUB):
            part = slice(b * SUB, (b + 1) * SUB)
            field = jnp.concatenate([ref[:, part, :].reshape(wide, nz) for ref in near], axis=0)
            mixed = dot(w_ref[...], field) + own[m][:, part, :].reshape(wide, nz).astype(F32)
            a_ref[b * wide : (b + 1) * wide, :] = mixed.astype(BF)
        result = dot(a_ref[...], m_ref[m]).astype(BF)
        for b in range(rows // SUB):
            for k in range(peers):
                piece = result[b * wide : (b + 1) * wide, k * block : (k + 1) * block]
                outs[k][at, :, b * SUB : (b + 1) * SUB, :] = piece.reshape(comp, SUB, block)


def couple_axial(peers, modes, x, before, after, weights, matrices):
    count, comp, rows, nz = x.shape
    return call(
        functools.partial(couple_axial_kernel, peers, modes, count, len(before)),
        "couple_axial",
        (x, *before, *after, weights, matrices),
        [shape(len(modes), comp, rows, nz // peers)] * peers,
        len(modes) * comp * rows * nz * 2 * (nz + 4 * comp * SUB),
        scratch=[pltpu.VMEM((comp * rows, nz), BF)],
    )


def radial_one(pieces, matrix, out):
    comp, _, block = pieces[0].shape
    for c in range(0, comp, 2):
        field = jnp.concatenate([jnp.concatenate([p[c], p[c + 1]], axis=1) for p in pieces], axis=0)
        result = dot(matrix, field).astype(BF)
        out[c] = result[:, :block]
        out[c + 1] = result[:, block:]


def radial_kernel(peers, modes, *refs):
    pieces, r_ref, outs = refs[:peers], refs[peers], refs[peers + 1 :]
    for at, m in enumerate(modes):
        radial_one([p.at[at] for p in pieces], r_ref[m], outs[at])


def radial(peers, modes, pieces, matrices):
    count, comp, rows, block = pieces[0].shape
    nr = rows * peers
    return call(
        functools.partial(radial_kernel, peers, modes),
        "radial",
        (*pieces, matrices),
        [shape(comp, nr, block)] * count,
        count * comp * nr * nr * block * 2,
    )


def radial_last_kernel(peers, *refs):
    radial_one([p.at[0] for p in refs[:peers]], refs[peers][0], refs[-1].at[0])


def radial_last(peers, first, total, pieces, matrices, partial_result):
    count, comp, rows, block = pieces[0].shape
    nr = rows * peers
    specs = [pl.BlockSpec((1, comp, rows, block), lambda i: (i, 0, 0, 0))] * peers
    specs.append(pl.BlockSpec((1, nr, nr), lambda i: (first + i, 0, 0)))
    args = [*pieces, matrices]
    aliases = {}
    if partial_result is not None:
        specs.append(pl.BlockSpec(memory_space=pl.ANY))
        aliases = {len(args): 0}
        args.append(partial_result)
    return pl.pallas_call(
        functools.partial(radial_last_kernel, peers),
        grid=(count,),
        out_shape=shape(total, comp, nr, block),
        in_specs=specs,
        out_specs=pl.BlockSpec((1, comp, nr, block), lambda i: (first + i, 0, 0, 0)),
        input_output_aliases=aliases,
        compiler_params=pltpu.CompilerParams(vmem_limit_bytes=VMEM_LIMIT),
        cost_estimate=pl.CostEstimate(
            flops=count * comp * nr * nr * block * 2,
            bytes_accessed=count * comp * nr * block * 4,
            transcendentals=0,
        ),
        name="radial_last",
    )(*args)


def couple_kernel(peers, modes, count, *refs):
    own, before, after = refs[:count], refs[count : count + 2], refs[count + 2 : count + 4]
    w_ref = refs[count + 4]
    outs = refs[count + 5 :]
    comp, nr, block = own[0].shape
    rows = nr // peers
    wide = comp * SUB
    for at, m in enumerate(modes):
        near = around(own, before, after, m)

        def side(ref, k):
            parts = [
                ref[:, k * rows + b * SUB : k * rows + (b + 1) * SUB, :].reshape(wide, block)
                for b in range(rows // SUB)
            ]
            return jnp.concatenate(parts, axis=1)

        for k in range(peers):
            field = jnp.concatenate([side(ref, k) for ref in near], axis=0)
            mixed = (dot(w_ref[...], field) + side(own[m], k).astype(F32)).astype(BF)
            for b in range(rows // SUB):
                piece = mixed[:, b * block : (b + 1) * block]
                outs[k][at, :, b * SUB : (b + 1) * SUB, :] = piece.reshape(comp, SUB, block)


def couple(peers, modes, own, before, after, weights):
    comp, nr, block = own[0].shape
    return call(
        functools.partial(couple_kernel, peers, modes, len(own)),
        "couple",
        (*own, *before, *after, weights),
        [shape(len(modes), comp, nr // peers, block)] * peers,
        len(modes) * comp * nr * block * 2 * 4 * comp * SUB,
    )


def axial_kernel(peers, modes, *refs):
    pieces, m_ref, outs = refs[:peers], refs[peers], refs[peers + 1 :]
    comp, rows, block = pieces[0].shape[1:]
    for at, m in enumerate(modes):
        field = jnp.concatenate([p[at].reshape(comp * rows, block) for p in pieces], axis=1)
        result = dot(field, m_ref[m]).astype(BF)
        for k in range(peers):
            outs[k][at] = result[:, k * block : (k + 1) * block].reshape(comp, rows, block)


def axial(peers, modes, pieces, matrices):
    count, comp, rows, block = pieces[0].shape
    nz = block * peers
    return call(
        functools.partial(axial_kernel, peers, modes),
        "axial",
        (*pieces, matrices),
        [shape(count, comp, rows, block)] * peers,
        count * comp * rows * nz * nz * 2,
    )


def swap(pieces):
    peers = len(pieces)
    result = list(pieces)
    for k in sorted(range(1, peers), key=lambda k: k == 1):
        result[k] = lax.ppermute(pieces[k], "pencil", [(i, i ^ k) for i in range(peers)])
    return result


def local(cotangent, radial_ops, lengths, couple_one, couple_two, axial_damping):
    peers, ring = lax.axis_size("pencil"), lax.axis_size("mode")
    up = [(i, (i + 1) % ring) for i in range(ring)]
    down = [(j, i) for i, j in up]
    count = cotangent.shape[0]
    modes = tuple(range(count))

    def send(plane, way):
        return lax.ppermute(plane, "mode", way)

    table = jnp.asarray(cosine_table(axial_damping.shape[1]))
    me = lax.axis_index("pencil").astype(jnp.int32).reshape(1)
    last = count - 1
    inner, outer = modes[1:last], (0, last)

    before = [send(cotangent[last], up)]
    after = [send(cotangent[0], down)]
    before.append(send(cotangent[last - 1], up))
    after.append(send(cotangent[1], down))
    m1, mpp, rpp, rp, weights = prepare(
        peers, me, lengths, table, axial_damping, radial_ops, couple_one, couple_two
    )
    inner_pieces = swap(couple_axial(peers, inner, cotangent, before[:1], after[:1], weights, m1))
    outer_pieces = swap(couple_axial(peers, outer, cotangent, before, after, weights, m1))
    planes = dict(zip(inner, radial(peers, inner, inner_pieces, rpp)))
    far_before, far_after = send(planes[last - 1], up), send(planes[1], down)
    planes.update(zip(outer, radial(peers, outer, outer_pieces, rpp)))
    before = [send(planes[last], up), far_before]
    after = [send(planes[0], down), far_after]
    planes = [planes[m] for m in modes]

    halves = (modes[: count // 2], modes[count // 2 :])
    pieces = [swap(couple(peers, half, planes, before, after, weights)) for half in halves]
    pieces = [swap(axial(peers, half, p, mpp)) for half, p in zip(halves, pieces)]
    result = None
    for half, p in zip(halves, pieces):
        result = radial_last(peers, half[0], count, p, rp, result)
    return result


def solution(mesh):
    return jax.shard_map(
        local,
        mesh=mesh,
        in_specs=(
            P("mode", None, "pencil", None),
            P("mode", None, None),
            P("mode"),
            P(),
            P(),
            P("mode", None),
        ),
        out_specs=P("mode", None, None, "pencil"),
        check_vma=False,
    )
```

```python
import functools
import math

import jax
import jax.numpy as jnp
import numpy as np
from jax import lax
from jax.experimental import pallas as pl
from jax.experimental.pallas import tpu as pltpu
from jax.sharding import PartitionSpec as P

BF = jnp.bfloat16
F32 = jnp.float32
SUB = 16
VMEM_LIMIT = 48 * 1024 * 1024


def cosine_table(count):
    points = np.arange(count, dtype=np.float32)
    scale = np.where(points == 0.0, np.float32(math.sqrt(1.0 / count)), np.float32(math.sqrt(2.0 / count)))
    angle = np.float32(math.pi) * (points[:, None] + np.float32(0.5)) * points[None, :] / np.float32(count)
    return (np.cos(angle).astype(np.float32) * scale[None, :].astype(np.float32)).astype(BF)


def vmem(count):
    return [pl.BlockSpec(memory_space=pltpu.VMEM)] * count


def call(kernel, name, args, outs, flops, scratch=(), smem=0):
    moved = sum(a.size * a.dtype.itemsize for a in args)
    moved += sum(math.prod(o.shape) * o.dtype.itemsize for o in outs)
    return pl.pallas_call(
        kernel,
        out_shape=outs,
        in_specs=[pl.BlockSpec(memory_space=pltpu.SMEM)] * smem + vmem(len(args) - smem),
        out_specs=vmem(len(outs)),
        scratch_shapes=list(scratch),
        compiler_params=pltpu.CompilerParams(vmem_limit_bytes=VMEM_LIMIT),
        cost_estimate=pl.CostEstimate(flops=flops, bytes_accessed=moved, transcendentals=0),
        name=name,
    )(*args)


def dot(a, b):
    return jnp.dot(a, b, preferred_element_type=F32)


def dot_nt(a, b):
    return lax.dot_general(a, b, (((1,), (1,)), ((), ())), preferred_element_type=F32)


def shape(*dims, dtype=BF):
    return jax.ShapeDtypeStruct(dims, dtype)


def prep_kernel(peers, order_ref, len_ref, q_ref, damp_ref, rad_ref, one_ref, two_ref, in_ref, out_ref, rin_ref, rout_ref, w_ref, qh_ref, qp_ref, turned_ref):
    nz = q_ref.shape[0]
    block = nz // peers
    for k in range(peers):
        for at, table in ((k, qh_ref), (peers + k, qp_ref)):
            start = pl.multiple_of(order_ref[at] * block, block)
            table[k * block : (k + 1) * block, :] = q_ref[pl.ds(start, block), :]
    for m in range(damp_ref.shape[0]):
        factor = damp_ref[m : m + 1, :]
        for left, right, out in ((qh_ref, q_ref, in_ref), (q_ref, qp_ref, out_ref)):
            scaled = left[...].astype(F32) * factor
            high = scaled.astype(BF)
            low = (scaled - high.astype(F32)).astype(BF)
            out[m] = (dot_nt(high, right[...]) + dot_nt(low, right[...])).astype(BF)
    nr = rad_ref.shape[1]
    rows = nr // peers
    for m in range(rad_ref.shape[0]):
        index = lax.broadcasted_iota(jnp.int32, (nr, nr), 0)
        turned_ref[...] = jnp.where(index < len_ref[m], rad_ref[m].astype(F32), 0.0).T.astype(BF)
        parts = []
        for k in range(peers):
            start = pl.multiple_of(order_ref[k] * rows, rows)
            rin_ref[m, k * rows : (k + 1) * rows, :] = turned_ref[pl.ds(start, rows), :]
            part = rad_ref[m, pl.ds(start, rows), :].astype(F32)
            index = start + lax.broadcasted_iota(jnp.int32, (rows, nr), 0)
            parts.append(jnp.where(index < len_ref[m], part, 0.0))
        rout_ref[m] = jnp.concatenate(parts, axis=0).T.astype(BF)
    comp = one_ref.shape[0]
    wide = comp * SUB
    row = lax.broadcasted_iota(jnp.int32, (wide, comp), 0) // SUB
    spread = jnp.where(row == lax.broadcasted_iota(jnp.int32, (wide, comp), 1), 1.0, 0.0).astype(BF)
    i = lax.broadcasted_iota(jnp.int32, (wide, wide), 0) % SUB
    j = lax.broadcasted_iota(jnp.int32, (wide, wide), 1) % SUB
    for at, ref in enumerate((one_ref, two_ref)):
        turned = ref[...].astype(BF).astype(F32)
        half = lax.dot_general(spread, turned.astype(BF), (((1,), (1,)), ((), ())), preferred_element_type=F32)
        full = dot_nt(half.astype(BF), spread)
        full = jnp.where(i == j, full, 0.0).astype(BF)
        w_ref[:, (2 * at) * wide : (2 * at + 1) * wide] = full
        w_ref[:, (2 * at + 1) * wide : (2 * at + 2) * wide] = full


def prepare(peers, order, lengths, table, damping, radial, one, two):
    modes, nz = damping.shape
    nr = radial.shape[1]
    wide = one.shape[0] * SUB
    return call(
        functools.partial(prep_kernel, peers),
        "prepare",
        (order, lengths, table, damping, radial, one, two),
        [
            shape(modes, nz, nz),
            shape(modes, nz, nz),
            shape(modes, nr, nr),
            shape(modes, nr, nr),
            shape(wide, 4 * wide),
        ],
        8 * modes * nz**3,
        scratch=[pltpu.VMEM((nz, nz), BF), pltpu.VMEM((nz, nz), BF), pltpu.VMEM((nr, nr), BF)],
        smem=2,
    )


def split_kernel(peers, order_ref, *refs):
    for k in range(peers):
        refs[peers + k][...] = refs[k][...]


def split(peers, order, x, first, step, number):
    _, comp, rows, nz = x.shape
    block = nz // peers
    return pl.pallas_call(
        functools.partial(split_kernel, peers),
        grid_spec=pltpu.PrefetchScalarGridSpec(
            num_scalar_prefetch=1,
            grid=(number,),
            in_specs=[
                pl.BlockSpec(
                    (1, comp, rows, block),
                    functools.partial(lambda k, i, order: (first + step * i, 0, 0, order[k]), k),
                )
                for k in range(peers)
            ],
            out_specs=[pl.BlockSpec((1, comp, rows, block), lambda i, order: (i, 0, 0, 0))] * peers,
        ),
        out_shape=[shape(number, comp, rows, block)] * peers,
        compiler_params=pltpu.CompilerParams(vmem_limit_bytes=VMEM_LIMIT),
        cost_estimate=pl.CostEstimate(
            flops=0, bytes_accessed=4 * number * comp * rows * nz, transcendentals=0
        ),
        name="split",
    )(order, *[x] * peers)


def by_parity(odd, given, taken):
    @pl.when(odd == 1)
    def _():
        taken[0][...] = given[0][...]
        taken[1][...] = given[1][...]

    @pl.when(odd == 0)
    def _():
        taken[0][...] = given[1][...]
        taken[1][...] = given[0][...]


def assemble_kernel(peers, order_ref, *refs):
    pieces, outs = refs[:peers], refs[peers:]
    rows = pieces[0].shape[2]
    for k in range(peers):
        start = pl.multiple_of(order_ref[peers + k] * rows, rows)
        for at, out in enumerate(outs[:2]):
            out[:, pl.ds(start, rows), :] = pieces[k][at]
    by_parity(order_ref[2 * peers], outs[:2], outs[2:])


def assemble(peers, order, pieces):
    count, comp, rows, block = pieces[0].shape
    return call(
        functools.partial(assemble_kernel, peers),
        "assemble",
        (order, *pieces),
        [shape(comp, rows * peers, block)] * 4,
        0,
        smem=1,
    )


def around(own, before, after, m):
    count = len(own)

    def at(i):
        if i < 0:
            return before[-1 - i]
        return own[i] if i < count else after[i - count]

    return [at(m - 1), at(m + 1), at(m - 2), at(m + 2)]


def couple_axial_kernel(peers, modes, count, depth, order_ref, *refs):
    own, refs = refs[:count], refs[count:]
    halos, refs = refs[: 2 * depth], refs[2 * depth :]
    sides = refs[3 + peers :]
    for i in range(0, 2 * depth, 2):
        by_parity(order_ref[2 * peers], halos[i : i + 2], sides[i : i + 2])
    before, after = sides[0::2], sides[1::2]
    w_ref, m_ref = refs[:2]
    outs, a_ref = refs[2 : 2 + peers], refs[2 + peers]
    comp, rows, nz = own[0].shape
    wide = comp * SUB
    block = nz // peers
    for at, m in enumerate(modes):
        near = around(own, before, after, m)
        for b in range(rows // SUB):
            part = slice(b * SUB, (b + 1) * SUB)
            field = jnp.concatenate([ref[:, part, :].reshape(wide, nz) for ref in near], axis=0)
            mixed = dot(w_ref[...], field) + own[m][:, part, :].reshape(wide, nz).astype(F32)
            a_ref[b * wide : (b + 1) * wide, :] = mixed.astype(BF)
        result = dot(a_ref[...], m_ref[m]).astype(BF)
        for b in range(rows // SUB):
            for k in range(peers):
                piece = result[b * wide : (b + 1) * wide, k * block : (k + 1) * block]
                outs[k][at, :, b * SUB : (b + 1) * SUB, :] = piece.reshape(comp, SUB, block)


def couple_axial(peers, order, modes, own, halos, weights, matrices):
    count = len(own)
    comp, rows, nz = own[0].shape
    return call(
        functools.partial(couple_axial_kernel, peers, modes, count, len(halos) // 2),
        "couple_axial",
        (order, *own, *halos, weights, matrices),
        [shape(len(modes), comp, rows, nz // peers)] * peers,
        len(modes) * comp * rows * nz * 2 * (nz + 4 * comp * SUB),
        scratch=[pltpu.VMEM((comp * rows, nz), BF)] + [pltpu.VMEM((comp, rows, nz), BF)] * len(halos),
        smem=1,
    )


def radial_one(pieces, matrix, out):
    comp, _, block = pieces[0].shape
    for c in range(0, comp, 2):
        field = jnp.concatenate([jnp.concatenate([p[c], p[c + 1]], axis=1) for p in pieces], axis=0)
        result = dot(matrix, field).astype(BF)
        out[c] = result[:, :block]
        out[c + 1] = result[:, block:]


def radial_last_kernel(peers, *refs):
    radial_one([p.at[0] for p in refs[:peers]], refs[peers][0], refs[-1].at[0])


def radial_last(peers, first, total, pieces, matrices, partial_result):
    count, comp, rows, block = pieces[0].shape
    nr = rows * peers
    specs = [pl.BlockSpec((1, comp, rows, block), lambda i: (i, 0, 0, 0))] * peers
    specs.append(pl.BlockSpec((1, nr, nr), lambda i: (first + i, 0, 0)))
    args = [*pieces, matrices]
    aliases = {}
    if partial_result is not None:
        specs.append(pl.BlockSpec(memory_space=pl.ANY))
        aliases = {len(args): 0}
        args.append(partial_result)
    return pl.pallas_call(
        functools.partial(radial_last_kernel, peers),
        grid=(count,),
        out_shape=shape(total, comp, nr, block),
        in_specs=specs,
        out_specs=pl.BlockSpec((1, comp, nr, block), lambda i: (first + i, 0, 0, 0)),
        input_output_aliases=aliases,
        compiler_params=pltpu.CompilerParams(vmem_limit_bytes=VMEM_LIMIT),
        cost_estimate=pl.CostEstimate(
            flops=count * comp * nr * nr * block * 2,
            bytes_accessed=count * comp * nr * block * 4,
            transcendentals=0,
        ),
        name="radial_last",
    )(*args)


def couple_radial_kernel(peers, modes, count, depth, order_ref, *refs):
    own, refs = refs[:count], refs[count:]
    halos, refs = refs[: 2 * depth], refs[2 * depth :]
    sides = refs[3 + peers :]
    for i in range(0, 2 * depth, 2):
        by_parity(order_ref[2 * peers], halos[i : i + 2], sides[i : i + 2])
    before, after = sides[0::2], sides[1::2]
    w_ref, r_ref = refs[:2]
    outs, a_ref = refs[2 : 2 + peers], refs[2 + peers]
    comp, nr, block = own[0].shape
    rows = nr // peers
    wide = comp * SUB
    for at, m in enumerate(modes):
        near = around(own, before, after, m)

        def side(ref, k):
            parts = [
                ref[:, k * rows + b * SUB : k * rows + (b + 1) * SUB, :].reshape(wide, block)
                for b in range(rows // SUB)
            ]
            return jnp.concatenate(parts, axis=1)

        for k in range(peers):
            field = jnp.concatenate([side(ref, k) for ref in near], axis=0)
            mixed = (dot(w_ref[...], field) + side(own[m], k).astype(F32)).astype(BF)
            for b in range(rows // SUB):
                piece = mixed[:, b * block : (b + 1) * block]
                a_ref[:, k * rows + b * SUB : k * rows + (b + 1) * SUB, :] = piece.reshape(comp, SUB, block)
        for c in range(0, comp, 2):
            field = jnp.concatenate([a_ref[c], a_ref[c + 1]], axis=1)
            result = dot(r_ref[m], field).astype(BF)
            for k in range(peers):
                part = slice(k * rows, (k + 1) * rows)
                outs[k][at, c] = result[part, :block]
                outs[k][at, c + 1] = result[part, block:]


def couple_radial(peers, order, modes, own, halos, weights, matrices):
    comp, nr, block = own[0].shape
    return call(
        functools.partial(couple_radial_kernel, peers, modes, len(own), len(halos) // 2),
        "couple_radial",
        (order, *own, *halos, weights, matrices),
        [shape(len(modes), comp, nr // peers, block)] * peers,
        len(modes) * comp * nr * block * 2 * (4 * comp * SUB + nr),
        scratch=[pltpu.VMEM((comp, nr, block), BF)] * (1 + len(halos)),
        smem=1,
    )


def axial_kernel(peers, modes, order_ref, *refs):
    pieces, m_ref, outs = refs[:peers], refs[peers], refs[peers + 1 :]
    comp, rows, block = pieces[0].shape[1:]
    for at, m in enumerate(modes):
        field = jnp.concatenate([p[at].reshape(comp * rows, block) for p in pieces], axis=1)
        outs[at][...] = dot(field, m_ref[m]).astype(BF).reshape(comp, rows, peers * block)
    by_parity(order_ref[2 * peers], outs[:2], outs[2:])


def axial(peers, order, modes, pieces, matrices):
    count, comp, rows, block = pieces[0].shape
    nz = block * peers
    return call(
        functools.partial(axial_kernel, peers, modes),
        "axial",
        (order, *pieces, matrices),
        [shape(comp, rows, nz)] * 4,
        count * comp * rows * nz * nz * 2,
        smem=1,
    )


def swap(pieces):
    peers = len(pieces)
    result = list(pieces)
    for k in sorted(range(1, peers), key=lambda k: k == 1):
        result[k] = lax.ppermute(pieces[k], "pencil", [(i, i ^ k) for i in range(peers)])
    return result


RUN = 8


def held(mode, peer):
    turned = (mode // RUN) % 2 * (peer % 2)
    return peer ^ (2 * turned)


def local(cotangent, radial_ops, lengths, couple_one, couple_two, axial_damping):
    peers, ring = lax.axis_size("pencil"), lax.axis_size("mode")
    pairs = ([], [])
    for mode in range(ring):
        beyond = (mode + 1) % ring
        for peer in range(peers):
            one, other = mode * peers + peer, beyond * peers + held(beyond, held(mode, peer))
            pairs[mode % 2].extend([(one, other), (other, one)])
    count = cotangent.shape[0]
    modes = tuple(range(count))

    def exchange(planes):
        return tuple(lax.ppermute(p, ("mode", "pencil"), pair) for p, pair in zip(planes, pairs))

    table = jnp.asarray(cosine_table(axial_damping.shape[1]))
    mode, me = lax.axis_index("mode"), lax.axis_index("pencil")
    others = me ^ jnp.arange(peers, dtype=jnp.int32)
    order = jnp.concatenate([held(mode, others), others, (mode % 2).reshape(1)]).astype(jnp.int32)
    last = count - 1
    inner, outer = (1, last - 1), (0, last)

    pieces_outer = swap(split(peers, order, cotangent, 0, last, 2))
    pieces_inner = split(peers, order, cotangent, 1, last - 2, 2)
    in_m, out_m, in_r, out_r, weights = prepare(
        peers, order, lengths, table, axial_damping, radial_ops, couple_one, couple_two
    )
    order, weights, pieces_inner, pieces_outer[2] = lax.optimization_barrier(
        (order, weights, pieces_inner, pieces_outer[2])
    )
    pieces_inner = swap(pieces_inner)
    low, high, *sent = assemble(peers, order, pieces_outer)
    near = exchange(sent)
    own = [low, *assemble(peers, order, pieces_inner), high]
    far = exchange(own[3:5])
    own = own[:3] + own[5:]
    pieces_inner = swap(couple_radial(peers, order, inner, own, near, weights, in_r))
    pieces_outer = swap(couple_radial(peers, order, outer, own, near + far, weights, in_r))
    low, high, *sent = axial(peers, order, inner, pieces_inner, in_m)
    far = exchange(sent)
    first, final, *sent = axial(peers, order, outer, pieces_outer, in_m)
    near = exchange(sent)
    own = [first, low, high, final]

    halves = (modes[: count // 2], modes[count // 2 :])
    pieces = [swap(couple_axial(peers, order, half, own, near + far, weights, out_m)) for half in halves]
    result = None
    for half, p in zip(halves, pieces):
        result = radial_last(peers, half[0], count, p, out_r, result)
    return result


def solution(mesh):
    return jax.shard_map(
        local,
        mesh=mesh,
        in_specs=(
            P("mode", None, "pencil", None),
            P("mode", None, None),
            P("mode"),
            P(),
            P(),
            P("mode", None),
        ),
        out_specs=P("mode", None, None, "pencil"),
        check_vma=False,
    )
```

```python
import functools
import math

import jax
import jax.numpy as jnp
import numpy as np
from jax import lax
from jax.experimental import pallas as pl
from jax.experimental.pallas import tpu as pltpu
from jax.sharding import PartitionSpec as P

BF = jnp.bfloat16
F32 = jnp.float32
SUB = 16
VMEM_LIMIT = 48 * 1024 * 1024


def cosine_table(count):
    points = np.arange(count, dtype=np.float32)
    scale = np.where(points == 0.0, np.float32(math.sqrt(1.0 / count)), np.float32(math.sqrt(2.0 / count)))
    angle = np.float32(math.pi) * (points[:, None] + np.float32(0.5)) * points[None, :] / np.float32(count)
    return (np.cos(angle).astype(np.float32) * scale[None, :].astype(np.float32)).astype(BF)


def vmem(count):
    return [pl.BlockSpec(memory_space=pltpu.VMEM)] * count


def call(kernel, name, args, outs, flops, scratch=(), smem=0):
    moved = sum(a.size * a.dtype.itemsize for a in args)
    moved += sum(math.prod(o.shape) * o.dtype.itemsize for o in outs)
    return pl.pallas_call(
        kernel,
        out_shape=outs,
        in_specs=[pl.BlockSpec(memory_space=pltpu.SMEM)] * smem + vmem(len(args) - smem),
        out_specs=vmem(len(outs)),
        scratch_shapes=list(scratch),
        compiler_params=pltpu.CompilerParams(vmem_limit_bytes=VMEM_LIMIT),
        cost_estimate=pl.CostEstimate(flops=flops, bytes_accessed=moved, transcendentals=0),
        name=name,
    )(*args)


def dot(a, b):
    return jnp.dot(a, b, preferred_element_type=F32)


def dot_nt(a, b):
    return lax.dot_general(a, b, (((1,), (1,)), ((), ())), preferred_element_type=F32)


def shape(*dims, dtype=BF):
    return jax.ShapeDtypeStruct(dims, dtype)


def prep_kernel(peers, order_ref, len_ref, q_ref, damp_ref, rad_ref, one_ref, two_ref, in_ref, out_ref, rin_ref, rout_ref, w_ref, qh_ref, qp_ref, turned_ref):
    nz = q_ref.shape[0]
    block = nz // peers
    for k in range(peers):
        for at, table in ((k, qh_ref), (peers + k, qp_ref)):
            start = pl.multiple_of(order_ref[at] * block, block)
            table[k * block : (k + 1) * block, :] = q_ref[pl.ds(start, block), :]
    for m in range(damp_ref.shape[0]):
        factor = damp_ref[m : m + 1, :]
        for left, right, out in ((qh_ref, q_ref, in_ref), (q_ref, qp_ref, out_ref)):
            scaled = left[...].astype(F32) * factor
            high = scaled.astype(BF)
            low = (scaled - high.astype(F32)).astype(BF)
            out[m] = (dot_nt(high, right[...]) + dot_nt(low, right[...])).astype(BF)
    nr = rad_ref.shape[1]
    rows = nr // peers
    for m in range(rad_ref.shape[0]):
        index = lax.broadcasted_iota(jnp.int32, (nr, nr), 0)
        turned_ref[...] = jnp.where(index < len_ref[m], rad_ref[m].astype(F32), 0.0).T.astype(BF)
        parts = []
        for k in range(peers):
            start = pl.multiple_of(order_ref[k] * rows, rows)
            rin_ref[m, k * rows : (k + 1) * rows, :] = turned_ref[pl.ds(start, rows), :]
            part = rad_ref[m, pl.ds(start, rows), :].astype(F32)
            index = start + lax.broadcasted_iota(jnp.int32, (rows, nr), 0)
            parts.append(jnp.where(index < len_ref[m], part, 0.0))
        rout_ref[m] = jnp.concatenate(parts, axis=0).T.astype(BF)
    comp = one_ref.shape[0]
    wide = comp * SUB
    row = lax.broadcasted_iota(jnp.int32, (wide, comp), 0) // SUB
    spread = jnp.where(row == lax.broadcasted_iota(jnp.int32, (wide, comp), 1), 1.0, 0.0).astype(BF)
    i = lax.broadcasted_iota(jnp.int32, (wide, wide), 0) % SUB
    j = lax.broadcasted_iota(jnp.int32, (wide, wide), 1) % SUB
    for at, ref in enumerate((one_ref, two_ref)):
        turned = ref[...].astype(BF).astype(F32)
        half = lax.dot_general(spread, turned.astype(BF), (((1,), (1,)), ((), ())), preferred_element_type=F32)
        full = dot_nt(half.astype(BF), spread)
        full = jnp.where(i == j, full, 0.0).astype(BF)
        w_ref[:, (2 * at) * wide : (2 * at + 1) * wide] = full
        w_ref[:, (2 * at + 1) * wide : (2 * at + 2) * wide] = full


def prepare(peers, order, lengths, table, damping, radial, one, two):
    modes, nz = damping.shape
    nr = radial.shape[1]
    wide = one.shape[0] * SUB
    return call(
        functools.partial(prep_kernel, peers),
        "prepare",
        (order, lengths, table, damping, radial, one, two),
        [
            shape(modes, nz, nz),
            shape(modes, nz, nz),
            shape(modes, nr, nr),
            shape(modes, nr, nr),
            shape(wide, 4 * wide),
        ],
        8 * modes * nz**3,
        scratch=[pltpu.VMEM((nz, nz), BF), pltpu.VMEM((nz, nz), BF), pltpu.VMEM((nr, nr), BF)],
        smem=2,
    )


def split_kernel(peers, order_ref, *refs):
    for k in range(peers):
        refs[peers + k][...] = refs[k][...]


def split(peers, order, x, first, step, number):
    _, comp, rows, nz = x.shape
    block = nz // peers
    return pl.pallas_call(
        functools.partial(split_kernel, peers),
        grid_spec=pltpu.PrefetchScalarGridSpec(
            num_scalar_prefetch=1,
            grid=(number,),
            in_specs=[
                pl.BlockSpec(
                    (1, comp, rows, block),
                    functools.partial(lambda k, i, order: (first + step * i, 0, 0, order[k]), k),
                )
                for k in range(peers)
            ],
            out_specs=[pl.BlockSpec((1, comp, rows, block), lambda i, order: (i, 0, 0, 0))] * peers,
        ),
        out_shape=[shape(number, comp, rows, block)] * peers,
        compiler_params=pltpu.CompilerParams(vmem_limit_bytes=VMEM_LIMIT),
        cost_estimate=pl.CostEstimate(
            flops=0, bytes_accessed=4 * number * comp * rows * nz, transcendentals=0
        ),
        name="split",
    )(order, *[x] * peers)


def by_parity(odd, given, taken):
    @pl.when(odd == 1)
    def _():
        taken[0][...] = given[0][...]
        taken[1][...] = given[1][...]

    @pl.when(odd == 0)
    def _():
        taken[0][...] = given[1][...]
        taken[1][...] = given[0][...]


def assemble_kernel(peers, order_ref, *refs):
    pieces, outs = refs[:peers], refs[peers:]
    rows = pieces[0].shape[2]
    for k in range(peers):
        start = pl.multiple_of(order_ref[peers + k] * rows, rows)
        for at, out in enumerate(outs[:2]):
            out[:, pl.ds(start, rows), :] = pieces[k][at]
    by_parity(order_ref[2 * peers], outs[:2], outs[2:])


def assemble(peers, order, pieces):
    count, comp, rows, block = pieces[0].shape
    return call(
        functools.partial(assemble_kernel, peers),
        "assemble",
        (order, *pieces),
        [shape(comp, rows * peers, block)] * 4,
        0,
        smem=1,
    )


def around(own, before, after, m):
    count = len(own)

    def at(i):
        if i < 0:
            return before[-1 - i]
        return own[i] if i < count else after[i - count]

    return [at(m - 1), at(m + 1), at(m - 2), at(m + 2)]


def couple_axial_kernel(peers, modes, count, depth, order_ref, *refs):
    own, refs = refs[:count], refs[count:]
    halos, refs = refs[: 2 * depth], refs[2 * depth :]
    sides = refs[3 + peers :]
    for i in range(0, 2 * depth, 2):
        by_parity(order_ref[2 * peers], halos[i : i + 2], sides[i : i + 2])
    before, after = sides[0::2], sides[1::2]
    w_ref, m_ref = refs[:2]
    outs, a_ref = refs[2 : 2 + peers], refs[2 + peers]
    comp, rows, nz = own[0].shape
    wide = comp * SUB
    block = nz // peers
    for at, m in enumerate(modes):
        near = around(own, before, after, m)
        for b in range(rows // SUB):
            part = slice(b * SUB, (b + 1) * SUB)
            field = jnp.concatenate([ref[:, part, :].reshape(wide, nz) for ref in near], axis=0)
            mixed = dot(w_ref[...], field) + own[m][:, part, :].reshape(wide, nz).astype(F32)
            a_ref[b * wide : (b + 1) * wide, :] = mixed.astype(BF)
        result = dot(a_ref[...], m_ref[m]).astype(BF)
        for b in range(rows // SUB):
            for k in range(peers):
                piece = result[b * wide : (b + 1) * wide, k * block : (k + 1) * block]
                outs[k][at, :, b * SUB : (b + 1) * SUB, :] = piece.reshape(comp, SUB, block)


def couple_axial(peers, order, modes, own, halos, weights, matrices):
    count = len(own)
    comp, rows, nz = own[0].shape
    return call(
        functools.partial(couple_axial_kernel, peers, modes, count, len(halos) // 2),
        "couple_axial",
        (order, *own, *halos, weights, matrices),
        [shape(len(modes), comp, rows, nz // peers)] * peers,
        len(modes) * comp * rows * nz * 2 * (nz + 4 * comp * SUB),
        scratch=[pltpu.VMEM((comp * rows, nz), BF)] + [pltpu.VMEM((comp, rows, nz), BF)] * len(halos),
        smem=1,
    )


def radial_one(pieces, matrix, out):
    comp, _, block = pieces[0].shape
    for c in range(0, comp, 2):
        field = jnp.concatenate([jnp.concatenate([p[c], p[c + 1]], axis=1) for p in pieces], axis=0)
        result = dot(matrix, field).astype(BF)
        out[c] = result[:, :block]
        out[c + 1] = result[:, block:]


def radial_last_kernel(peers, *refs):
    radial_one([p.at[0] for p in refs[:peers]], refs[peers][0], refs[-1].at[0])


def radial_last(peers, modes, total, pieces, matrices, partial_result):
    count, comp, rows, block = pieces[0].shape
    first, step = modes[0], modes[1] - modes[0]
    nr = rows * peers
    specs = [pl.BlockSpec((1, comp, rows, block), lambda i: (i, 0, 0, 0))] * peers
    specs.append(pl.BlockSpec((1, nr, nr), lambda i: (first + step * i, 0, 0)))
    args = [*pieces, matrices]
    aliases = {}
    if partial_result is not None:
        specs.append(pl.BlockSpec(memory_space=pl.ANY))
        aliases = {len(args): 0}
        args.append(partial_result)
    return pl.pallas_call(
        functools.partial(radial_last_kernel, peers),
        grid=(count,),
        out_shape=shape(total, comp, nr, block),
        in_specs=specs,
        out_specs=pl.BlockSpec((1, comp, nr, block), lambda i: (first + step * i, 0, 0, 0)),
        input_output_aliases=aliases,
        compiler_params=pltpu.CompilerParams(vmem_limit_bytes=VMEM_LIMIT),
        cost_estimate=pl.CostEstimate(
            flops=count * comp * nr * nr * block * 2,
            bytes_accessed=count * comp * nr * block * 4,
            transcendentals=0,
        ),
        name="radial_last",
    )(*args)


def couple_radial_kernel(peers, modes, count, depth, order_ref, *refs):
    own, refs = refs[:count], refs[count:]
    halos, refs = refs[: 2 * depth], refs[2 * depth :]
    sides = refs[3 + peers :]
    for i in range(0, 2 * depth, 2):
        by_parity(order_ref[2 * peers], halos[i : i + 2], sides[i : i + 2])
    before, after = sides[0::2], sides[1::2]
    w_ref, r_ref = refs[:2]
    outs, a_ref = refs[2 : 2 + peers], refs[2 + peers]
    comp, nr, block = own[0].shape
    rows = nr // peers
    wide = comp * SUB
    for at, m in enumerate(modes):
        near = around(own, before, after, m)

        def side(ref, k):
            parts = [
                ref[:, k * rows + b * SUB : k * rows + (b + 1) * SUB, :].reshape(wide, block)
                for b in range(rows // SUB)
            ]
            return jnp.concatenate(parts, axis=1)

        for k in range(peers):
            field = jnp.concatenate([side(ref, k) for ref in near], axis=0)
            mixed = (dot(w_ref[...], field) + side(own[m], k).astype(F32)).astype(BF)
            for b in range(rows // SUB):
                piece = mixed[:, b * block : (b + 1) * block]
                a_ref[:, k * rows + b * SUB : k * rows + (b + 1) * SUB, :] = piece.reshape(comp, SUB, block)
        for c in range(0, comp, 2):
            field = jnp.concatenate([a_ref[c], a_ref[c + 1]], axis=1)
            result = dot(r_ref[m], field).astype(BF)
            for k in range(peers):
                part = slice(k * rows, (k + 1) * rows)
                outs[k][at, c] = result[part, :block]
                outs[k][at, c + 1] = result[part, block:]


def couple_radial(peers, order, modes, own, halos, weights, matrices):
    comp, nr, block = own[0].shape
    return call(
        functools.partial(couple_radial_kernel, peers, modes, len(own), len(halos) // 2),
        "couple_radial",
        (order, *own, *halos, weights, matrices),
        [shape(len(modes), comp, nr // peers, block)] * peers,
        len(modes) * comp * nr * block * 2 * (4 * comp * SUB + nr),
        scratch=[pltpu.VMEM((comp, nr, block), BF)] * (1 + len(halos)),
        smem=1,
    )


def axial_kernel(peers, modes, order_ref, *refs):
    pieces, m_ref, outs = refs[:peers], refs[peers], refs[peers + 1 :]
    comp, rows, block = pieces[0].shape[1:]
    for at, m in enumerate(modes):
        field = jnp.concatenate([p[at].reshape(comp * rows, block) for p in pieces], axis=1)
        outs[at][...] = dot(field, m_ref[m]).astype(BF).reshape(comp, rows, peers * block)
    by_parity(order_ref[2 * peers], outs[:2], outs[2:])


def axial(peers, order, modes, pieces, matrices):
    count, comp, rows, block = pieces[0].shape
    nz = block * peers
    return call(
        functools.partial(axial_kernel, peers, modes),
        "axial",
        (order, *pieces, matrices),
        [shape(comp, rows, nz)] * 4,
        count * comp * rows * nz * nz * 2,
        smem=1,
    )


def swap(pieces):
    peers = len(pieces)
    result = list(pieces)
    for k in sorted(range(1, peers), key=lambda k: k == 1):
        result[k] = lax.ppermute(pieces[k], "pencil", [(i, i ^ k) for i in range(peers)])
    return result


RUN = 8


def held(mode, peer):
    turned = (mode // RUN) % 2 * (peer % 2)
    return peer ^ (2 * turned)


def local(cotangent, radial_ops, lengths, couple_one, couple_two, axial_damping):
    peers, ring = lax.axis_size("pencil"), lax.axis_size("mode")
    pairs = ([], [])
    for mode in range(ring):
        beyond = (mode + 1) % ring
        for peer in range(peers):
            one, other = mode * peers + peer, beyond * peers + held(beyond, held(mode, peer))
            pairs[mode % 2].extend([(one, other), (other, one)])
    count = cotangent.shape[0]
    modes = tuple(range(count))

    def exchange(planes):
        return tuple(lax.ppermute(p, ("mode", "pencil"), pair) for p, pair in zip(planes, pairs))

    table = jnp.asarray(cosine_table(axial_damping.shape[1]))
    mode, me = lax.axis_index("mode"), lax.axis_index("pencil")
    others = me ^ jnp.arange(peers, dtype=jnp.int32)
    order = jnp.concatenate([held(mode, others), others, (mode % 2).reshape(1)]).astype(jnp.int32)
    last = count - 1
    inner, outer = (1, last - 1), (0, last)

    pieces_outer = swap(split(peers, order, cotangent, 0, last, 2))
    pieces_inner = split(peers, order, cotangent, 1, last - 2, 2)
    in_m, out_m, in_r, out_r, weights = prepare(
        peers, order, lengths, table, axial_damping, radial_ops, couple_one, couple_two
    )
    order, weights, pieces_inner, pieces_outer[2] = lax.optimization_barrier(
        (order, weights, pieces_inner, pieces_outer[2])
    )
    pieces_inner = swap(pieces_inner)
    low, high, *sent = assemble(peers, order, pieces_outer)
    near = exchange(sent)
    own = [low, *assemble(peers, order, pieces_inner), high]
    far = exchange(own[3:5])
    own = own[:3] + own[5:]
    pieces_inner = swap(couple_radial(peers, order, inner, own, near, weights, in_r))
    pieces_outer = swap(couple_radial(peers, order, outer, own, near + far, weights, in_r))
    low, high, *far = axial(peers, order, inner, pieces_inner, in_m)
    first, final, *near = axial(peers, order, outer, pieces_outer, in_m)
    near, far = lax.optimization_barrier((near, far))
    near, far = exchange(near), exchange(far)
    own = [first, low, high, final]
    pieces_inner = swap(couple_axial(peers, order, inner, own, near, weights, out_m))
    pieces_outer = swap(couple_axial(peers, order, outer, own, near + far, weights, out_m))
    result = radial_last(peers, inner, count, pieces_inner, out_r, None)
    result = radial_last(peers, outer, count, pieces_outer, out_r, result)
    return result


def solution(mesh):
    return jax.shard_map(
        local,
        mesh=mesh,
        in_specs=(
            P("mode", None, "pencil", None),
            P("mode", None, None),
            P("mode"),
            P(),
            P(),
            P("mode", None),
        ),
        out_specs=P("mode", None, None, "pencil"),
        check_vma=False,
    )
```

```python
import functools
import math

import jax
import jax.numpy as jnp
import numpy as np
from jax import lax
from jax.experimental import pallas as pl
from jax.experimental.pallas import tpu as pltpu
from jax.sharding import PartitionSpec as P

BF = jnp.bfloat16
F32 = jnp.float32
SUB = 16
VMEM_LIMIT = 16 * 1024 * 1024


def cosine_table(count):
    points = np.arange(count, dtype=np.float32)
    scale = np.where(points == 0.0, np.float32(math.sqrt(1.0 / count)), np.float32(math.sqrt(2.0 / count)))
    angle = np.float32(math.pi) * (points[:, None] + np.float32(0.5)) * points[None, :] / np.float32(count)
    return (np.cos(angle).astype(np.float32) * scale[None, :].astype(np.float32)).astype(BF)


def vmem(count):
    return [pl.BlockSpec(memory_space=pltpu.VMEM)] * count


def call(kernel, name, args, outs, flops, scratch=(), smem=0):
    moved = sum(a.size * a.dtype.itemsize for a in args)
    moved += sum(math.prod(o.shape) * o.dtype.itemsize for o in outs)
    return pl.pallas_call(
        kernel,
        out_shape=outs,
        in_specs=[pl.BlockSpec(memory_space=pltpu.SMEM)] * smem + vmem(len(args) - smem),
        out_specs=vmem(len(outs)),
        scratch_shapes=list(scratch),
        compiler_params=pltpu.CompilerParams(vmem_limit_bytes=VMEM_LIMIT),
        cost_estimate=pl.CostEstimate(flops=flops, bytes_accessed=moved, transcendentals=0),
        name=name,
    )(*args)


def dot(a, b):
    return jnp.dot(a, b, preferred_element_type=F32)


def dot_nt(a, b):
    return lax.dot_general(a, b, (((1,), (1,)), ((), ())), preferred_element_type=F32)


def shape(*dims, dtype=BF):
    return jax.ShapeDtypeStruct(dims, dtype)


def prep_kernel(peers, order_ref, len_ref, q_ref, damp_ref, rad_ref, one_ref, two_ref, in_ref, out_ref, rin_ref, rout_ref, w_ref, qh_ref, qp_ref, turned_ref):
    nz = q_ref.shape[0]
    block = nz // peers
    for k in range(peers):
        for at, table in ((k, qh_ref), (peers + k, qp_ref)):
            start = pl.multiple_of(order_ref[at] * block, block)
            table[k * block : (k + 1) * block, :] = q_ref[pl.ds(start, block), :]
    for m in range(damp_ref.shape[0]):
        factor = damp_ref[m : m + 1, :]
        for left, right, out in ((qh_ref, q_ref, in_ref), (q_ref, qp_ref, out_ref)):
            scaled = left[...].astype(F32) * factor
            high = scaled.astype(BF)
            low = (scaled - high.astype(F32)).astype(BF)
            out[m] = (dot_nt(high, right[...]) + dot_nt(low, right[...])).astype(BF)
    nr = rad_ref.shape[1]
    rows = nr // peers
    for m in range(rad_ref.shape[0]):
        index = lax.broadcasted_iota(jnp.int32, (nr, nr), 0)
        turned_ref[...] = jnp.where(index < len_ref[m], rad_ref[m].astype(F32), 0.0).T.astype(BF)
        parts = []
        for k in range(peers):
            start = pl.multiple_of(order_ref[k] * rows, rows)
            rin_ref[m, k * rows : (k + 1) * rows, :] = turned_ref[pl.ds(start, rows), :]
            part = rad_ref[m, pl.ds(start, rows), :].astype(F32)
            index = start + lax.broadcasted_iota(jnp.int32, (rows, nr), 0)
            parts.append(jnp.where(index < len_ref[m], part, 0.0))
        rout_ref[m] = jnp.concatenate(parts, axis=0).T.astype(BF)
    comp = one_ref.shape[0]
    wide = comp * SUB
    row = lax.broadcasted_iota(jnp.int32, (wide, comp), 0) // SUB
    spread = jnp.where(row == lax.broadcasted_iota(jnp.int32, (wide, comp), 1), 1.0, 0.0).astype(BF)
    i = lax.broadcasted_iota(jnp.int32, (wide, wide), 0) % SUB
    j = lax.broadcasted_iota(jnp.int32, (wide, wide), 1) % SUB
    for at, ref in enumerate((one_ref, two_ref)):
        turned = ref[...].astype(BF).astype(F32)
        half = lax.dot_general(spread, turned.astype(BF), (((1,), (1,)), ((), ())), preferred_element_type=F32)
        full = dot_nt(half.astype(BF), spread)
        full = jnp.where(i == j, full, 0.0).astype(BF)
        w_ref[:, (2 * at) * wide : (2 * at + 1) * wide] = full
        w_ref[:, (2 * at + 1) * wide : (2 * at + 2) * wide] = full


def prepare(peers, order, lengths, table, damping, radial, one, two):
    modes, nz = damping.shape
    nr = radial.shape[1]
    wide = one.shape[0] * SUB
    return call(
        functools.partial(prep_kernel, peers),
        "prepare",
        (order, lengths, table, damping, radial, one, two),
        [
            shape(modes, nz, nz),
            shape(modes, nz, nz),
            shape(modes, nr, nr),
            shape(modes, nr, nr),
            shape(wide, 4 * wide),
        ],
        8 * modes * nz**3,
        scratch=[pltpu.VMEM((nz, nz), BF), pltpu.VMEM((nz, nz), BF), pltpu.VMEM((nr, nr), BF)],
        smem=2,
    )


def split_kernel(peers, order_ref, *refs):
    for k in range(peers):
        refs[peers + k][...] = refs[k][...]


def split(peers, order, x, first, step, number):
    _, comp, rows, nz = x.shape
    block = nz // peers
    return pl.pallas_call(
        functools.partial(split_kernel, peers),
        grid_spec=pltpu.PrefetchScalarGridSpec(
            num_scalar_prefetch=1,
            grid=(number,),
            in_specs=[
                pl.BlockSpec(
                    (1, comp, rows, block),
                    functools.partial(lambda k, i, order: (first + step * i, 0, 0, order[k]), k),
                )
                for k in range(peers)
            ],
            out_specs=[pl.BlockSpec((1, comp, rows, block), lambda i, order: (i, 0, 0, 0))] * peers,
        ),
        out_shape=[shape(number, comp, rows, block)] * peers,
        compiler_params=pltpu.CompilerParams(vmem_limit_bytes=VMEM_LIMIT),
        cost_estimate=pl.CostEstimate(
            flops=0, bytes_accessed=4 * number * comp * rows * nz, transcendentals=0
        ),
        name="split",
    )(order, *[x] * peers)


def by_parity(odd, given, taken):
    @pl.when(odd == 1)
    def _():
        taken[0][...] = given[0][...]
        taken[1][...] = given[1][...]

    @pl.when(odd == 0)
    def _():
        taken[0][...] = given[1][...]
        taken[1][...] = given[0][...]


def assemble_kernel(peers, order_ref, *refs):
    pieces, outs = refs[:peers], refs[peers:]
    rows = pieces[0].shape[2]
    for k in range(peers):
        start = pl.multiple_of(order_ref[peers + k] * rows, rows)
        for at, out in enumerate(outs[:2]):
            out[:, pl.ds(start, rows), :] = pieces[k][at]
    by_parity(order_ref[2 * peers], outs[:2], outs[2:])


def assemble(peers, order, pieces):
    count, comp, rows, block = pieces[0].shape
    return call(
        functools.partial(assemble_kernel, peers),
        "assemble",
        (order, *pieces),
        [shape(comp, rows * peers, block)] * 4,
        0,
        smem=1,
    )


class Chosen:
    def __init__(self, flag, one, other):
        self.flag, self.one, self.other = flag, one, other

    def __getitem__(self, at):
        return jnp.where(self.flag, self.one[at], self.other[at])


def around(own, before, after, m):
    count = len(own)

    def at(i):
        if i < 0:
            return before[-1 - i]
        return own[i] if i < count else after[i - count]

    return [at(m - 1), at(m + 1), at(m - 2), at(m + 2)]


def couple_axial_kernel(peers, modes, count, depth, order_ref, *refs):
    own, refs = refs[:count], refs[count:]
    halos, refs = refs[: 2 * depth], refs[2 * depth :]
    odd = order_ref[2 * peers] == 1
    before = [Chosen(odd, *halos[i : i + 2]) for i in range(0, 2 * depth, 2)]
    after = [Chosen(odd, *halos[i : i + 2][::-1]) for i in range(0, 2 * depth, 2)]
    w_ref, m_ref = refs[:2]
    outs, a_ref = refs[2 : 2 + peers], refs[2 + peers]
    comp, rows, nz = own[0].shape
    wide = comp * SUB
    block = nz // peers
    for at, m in enumerate(modes):
        near = around(own, before, after, m)
        for b in range(rows // SUB):
            part = slice(b * SUB, (b + 1) * SUB)
            field = jnp.concatenate([ref[:, part, :].reshape(wide, nz) for ref in near], axis=0)
            mixed = dot(w_ref[...], field) + own[m][:, part, :].reshape(wide, nz).astype(F32)
            a_ref[b * wide : (b + 1) * wide, :] = mixed.astype(BF)
        result = dot(a_ref[...], m_ref[m]).astype(BF)
        for b in range(rows // SUB):
            for k in range(peers):
                piece = result[b * wide : (b + 1) * wide, k * block : (k + 1) * block]
                outs[k][at, :, b * SUB : (b + 1) * SUB, :] = piece.reshape(comp, SUB, block)


def couple_axial(peers, order, modes, own, halos, weights, matrices):
    count = len(own)
    comp, rows, nz = own[0].shape
    return call(
        functools.partial(couple_axial_kernel, peers, modes, count, len(halos) // 2),
        "couple_axial",
        (order, *own, *halos, weights, matrices),
        [shape(len(modes), comp, rows, nz // peers)] * peers,
        len(modes) * comp * rows * nz * 2 * (nz + 4 * comp * SUB),
        scratch=[pltpu.VMEM((comp * rows, nz), BF)],
        smem=1,
    )


def radial_one(pieces, matrix, out):
    comp, _, block = pieces[0].shape
    for c in range(0, comp, 2):
        field = jnp.concatenate([jnp.concatenate([p[c], p[c + 1]], axis=1) for p in pieces], axis=0)
        result = dot(matrix, field).astype(BF)
        out[c] = result[:, :block]
        out[c + 1] = result[:, block:]


def radial_last_kernel(peers, *refs):
    radial_one([p.at[0] for p in refs[:peers]], refs[peers][0], refs[-1].at[0])


def radial_last(peers, modes, total, pieces, matrices, partial_result):
    count, comp, rows, block = pieces[0].shape
    first, step = modes[0], modes[1] - modes[0]
    nr = rows * peers
    specs = [pl.BlockSpec((1, comp, rows, block), lambda i: (i, 0, 0, 0))] * peers
    specs.append(pl.BlockSpec((1, nr, nr), lambda i: (first + step * i, 0, 0)))
    args = [*pieces, matrices]
    aliases = {}
    if partial_result is not None:
        specs.append(pl.BlockSpec(memory_space=pl.ANY))
        aliases = {len(args): 0}
        args.append(partial_result)
    return pl.pallas_call(
        functools.partial(radial_last_kernel, peers),
        grid=(count,),
        out_shape=shape(total, comp, nr, block),
        in_specs=specs,
        out_specs=pl.BlockSpec((1, comp, nr, block), lambda i: (first + step * i, 0, 0, 0)),
        input_output_aliases=aliases,
        compiler_params=pltpu.CompilerParams(vmem_limit_bytes=VMEM_LIMIT),
        cost_estimate=pl.CostEstimate(
            flops=count * comp * nr * nr * block * 2,
            bytes_accessed=count * comp * nr * block * 4,
            transcendentals=0,
        ),
        name="radial_last",
    )(*args)


def couple_radial_kernel(peers, modes, count, depth, order_ref, *refs):
    own, refs = refs[:count], refs[count:]
    halos, refs = refs[: 2 * depth], refs[2 * depth :]
    odd = order_ref[2 * peers] == 1
    before = [Chosen(odd, *halos[i : i + 2]) for i in range(0, 2 * depth, 2)]
    after = [Chosen(odd, *halos[i : i + 2][::-1]) for i in range(0, 2 * depth, 2)]
    w_ref, r_ref = refs[:2]
    outs, a_ref = refs[2 : 2 + peers], refs[2 + peers]
    comp, nr, block = own[0].shape
    rows = nr // peers
    wide = comp * SUB
    for at, m in enumerate(modes):
        near = around(own, before, after, m)

        def side(ref, k):
            parts = [
                ref[:, k * rows + b * SUB : k * rows + (b + 1) * SUB, :].reshape(wide, block)
                for b in range(rows // SUB)
            ]
            return jnp.concatenate(parts, axis=1)

        for k in range(peers):
            field = jnp.concatenate([side(ref, k) for ref in near], axis=0)
            mixed = (dot(w_ref[...], field) + side(own[m], k).astype(F32)).astype(BF)
            for b in range(rows // SUB):
                piece = mixed[:, b * block : (b + 1) * block]
                a_ref[:, k * rows + b * SUB : k * rows + (b + 1) * SUB, :] = piece.reshape(comp, SUB, block)
        for c in range(0, comp, 2):
            field = jnp.concatenate([a_ref[c], a_ref[c + 1]], axis=1)
            result = dot(r_ref[m], field).astype(BF)
            for k in range(peers):
                part = slice(k * rows, (k + 1) * rows)
                outs[k][at, c] = result[part, :block]
                outs[k][at, c + 1] = result[part, block:]


def couple_radial(peers, order, modes, own, halos, weights, matrices):
    comp, nr, block = own[0].shape
    return call(
        functools.partial(couple_radial_kernel, peers, modes, len(own), len(halos) // 2),
        "couple_radial",
        (order, *own, *halos, weights, matrices),
        [shape(len(modes), comp, nr // peers, block)] * peers,
        len(modes) * comp * nr * block * 2 * (4 * comp * SUB + nr),
        scratch=[pltpu.VMEM((comp, nr, block), BF)],
        smem=1,
    )


def axial_kernel(peers, modes, order_ref, *refs):
    pieces, m_ref, outs = refs[:peers], refs[peers], refs[peers + 1 :]
    comp, rows, block = pieces[0].shape[1:]
    for at, m in enumerate(modes):
        field = jnp.concatenate([p[at].reshape(comp * rows, block) for p in pieces], axis=1)
        outs[at][...] = dot(field, m_ref[m]).astype(BF).reshape(comp, rows, peers * block)
    by_parity(order_ref[2 * peers], outs[:2], outs[2:])


def axial(peers, order, modes, pieces, matrices):
    count, comp, rows, block = pieces[0].shape
    nz = block * peers
    return call(
        functools.partial(axial_kernel, peers, modes),
        "axial",
        (order, *pieces, matrices),
        [shape(comp, rows, nz)] * 4,
        count * comp * rows * nz * nz * 2,
        smem=1,
    )


def swap(pieces):
    peers = len(pieces)
    result = list(pieces)
    for k in sorted(range(1, peers), key=lambda k: k == 1):
        result[k] = lax.ppermute(pieces[k], "pencil", [(i, i ^ k) for i in range(peers)])
    return result


RUN = 8


def held(mode, peer):
    turned = (mode // RUN) % 2 * (peer % 2)
    return peer ^ (2 * turned)


def local(cotangent, radial_ops, lengths, couple_one, couple_two, axial_damping):
    peers, ring = lax.axis_size("pencil"), lax.axis_size("mode")
    pairs = ([], [])
    for mode in range(ring):
        beyond = (mode + 1) % ring
        for peer in range(peers):
            one, other = mode * peers + peer, beyond * peers + held(beyond, held(mode, peer))
            pairs[mode % 2].extend([(one, other), (other, one)])
    count = cotangent.shape[0]
    modes = tuple(range(count))

    def exchange(planes):
        return tuple(lax.ppermute(p, ("mode", "pencil"), pair) for p, pair in zip(planes, pairs))

    table = jnp.asarray(cosine_table(axial_damping.shape[1]))
    mode, me = lax.axis_index("mode"), lax.axis_index("pencil")
    others = me ^ jnp.arange(peers, dtype=jnp.int32)
    order = jnp.concatenate([held(mode, others), others, (mode % 2).reshape(1)]).astype(jnp.int32)
    last = count - 1
    inner, outer = (1, last - 1), (0, last)

    pieces_outer = swap(split(peers, order, cotangent, 0, last, 2))
    pieces_inner = split(peers, order, cotangent, 1, last - 2, 2)
    in_m, out_m, in_r, out_r, weights = prepare(
        peers, order, lengths, table, axial_damping, radial_ops, couple_one, couple_two
    )
    order, weights, pieces_inner, pieces_outer[2] = lax.optimization_barrier(
        (order, weights, pieces_inner, pieces_outer[2])
    )
    pieces_inner = swap(pieces_inner)
    low, high, *sent = assemble(peers, order, pieces_outer)
    near = exchange(sent)
    own = [low, *assemble(peers, order, pieces_inner), high]
    far = exchange(own[3:5])
    own = own[:3] + own[5:]
    pieces_inner = swap(couple_radial(peers, order, inner, own, near, weights, in_r))
    pieces_outer = swap(couple_radial(peers, order, outer, own, near + far, weights, in_r))
    low, high, *far = axial(peers, order, inner, pieces_inner, in_m)
    first, final, *near = axial(peers, order, outer, pieces_outer, in_m)
    near, far = lax.optimization_barrier((near, far))
    near, far = exchange(near), exchange(far)
    own = [first, low, high, final]
    pieces_inner = swap(couple_axial(peers, order, inner, own, near, weights, out_m))
    pieces_outer = swap(couple_axial(peers, order, outer, own, near + far, weights, out_m))
    result = radial_last(peers, inner, count, pieces_inner, out_r, None)
    result = radial_last(peers, outer, count, pieces_outer, out_r, result)
    return result


def solution(mesh):
    return jax.shard_map(
        local,
        mesh=mesh,
        in_specs=(
            P("mode", None, "pencil", None),
            P("mode", None, None),
            P("mode"),
            P(),
            P(),
            P("mode", None),
        ),
        out_specs=P("mode", None, None, "pencil"),
        check_vma=False,
    )
```

```python
import functools
import math

import jax
import jax.numpy as jnp
import numpy as np
from jax import lax
from jax.experimental import pallas as pl
from jax.experimental.pallas import tpu as pltpu
from jax.sharding import PartitionSpec as P

BF = jnp.bfloat16
F32 = jnp.float32
SUB = 16
VMEM_LIMIT = 16 * 1024 * 1024


def cosine_table(count):
    points = np.arange(count, dtype=np.float32)
    scale = np.where(points == 0.0, np.float32(math.sqrt(1.0 / count)), np.float32(math.sqrt(2.0 / count)))
    angle = np.float32(math.pi) * (points[:, None] + np.float32(0.5)) * points[None, :] / np.float32(count)
    return (np.cos(angle).astype(np.float32) * scale[None, :].astype(np.float32)).astype(BF)


def vmem(count):
    return [pl.BlockSpec(memory_space=pltpu.VMEM)] * count


def call(kernel, name, args, outs, flops, scratch=(), smem=0):
    moved = sum(a.size * a.dtype.itemsize for a in args)
    moved += sum(math.prod(o.shape) * o.dtype.itemsize for o in outs)
    return pl.pallas_call(
        kernel,
        out_shape=outs,
        in_specs=[pl.BlockSpec(memory_space=pltpu.SMEM)] * smem + vmem(len(args) - smem),
        out_specs=vmem(len(outs)),
        scratch_shapes=list(scratch),
        compiler_params=pltpu.CompilerParams(vmem_limit_bytes=VMEM_LIMIT),
        cost_estimate=pl.CostEstimate(flops=flops, bytes_accessed=moved, transcendentals=0),
        name=name,
    )(*args)


def dot(a, b):
    return jnp.dot(a, b, preferred_element_type=F32)


def dot_nt(a, b):
    return lax.dot_general(a, b, (((1,), (1,)), ((), ())), preferred_element_type=F32)


def shape(*dims, dtype=BF):
    return jax.ShapeDtypeStruct(dims, dtype)


def prep_kernel(peers, order_ref, len_ref, q_ref, damp_ref, rad_ref, one_ref, two_ref, in_ref, out_ref, rin_ref, rout_ref, w_ref, qh_ref, qp_ref, turned_ref):
    nz = q_ref.shape[0]
    block = nz // peers
    for k in range(peers):
        for at, table in ((k, qh_ref), (peers + k, qp_ref)):
            start = pl.multiple_of(order_ref[at] * block, block)
            table[k * block : (k + 1) * block, :] = q_ref[pl.ds(start, block), :]
    for m in range(damp_ref.shape[0]):
        factor = damp_ref[m : m + 1, :]
        for left, right, out in ((qh_ref, q_ref, in_ref), (q_ref, qp_ref, out_ref)):
            scaled = left[...].astype(F32) * factor
            high = scaled.astype(BF)
            low = (scaled - high.astype(F32)).astype(BF)
            out[m] = (dot_nt(high, right[...]) + dot_nt(low, right[...])).astype(BF)
    nr = rad_ref.shape[1]
    rows = nr // peers
    for m in range(rad_ref.shape[0]):
        index = lax.broadcasted_iota(jnp.int32, (nr, nr), 0)
        turned_ref[...] = jnp.where(index < len_ref[m], rad_ref[m].astype(F32), 0.0).T.astype(BF)
        parts = []
        for k in range(peers):
            start = pl.multiple_of(order_ref[k] * rows, rows)
            rin_ref[m, k * rows : (k + 1) * rows, :] = turned_ref[pl.ds(start, rows), :]
            part = rad_ref[m, pl.ds(start, rows), :].astype(F32)
            index = start + lax.broadcasted_iota(jnp.int32, (rows, nr), 0)
            parts.append(jnp.where(index < len_ref[m], part, 0.0))
        rout_ref[m] = jnp.concatenate(parts, axis=0).T.astype(BF)
    comp = one_ref.shape[0]
    wide = comp * SUB
    row = lax.broadcasted_iota(jnp.int32, (wide, comp), 0) // SUB
    spread = jnp.where(row == lax.broadcasted_iota(jnp.int32, (wide, comp), 1), 1.0, 0.0).astype(BF)
    i = lax.broadcasted_iota(jnp.int32, (wide, wide), 0) % SUB
    j = lax.broadcasted_iota(jnp.int32, (wide, wide), 1) % SUB
    for at, ref in enumerate((one_ref, two_ref)):
        turned = ref[...].astype(BF).astype(F32)
        half = lax.dot_general(spread, turned.astype(BF), (((1,), (1,)), ((), ())), preferred_element_type=F32)
        full = dot_nt(half.astype(BF), spread)
        full = jnp.where(i == j, full, 0.0).astype(BF)
        w_ref[:, (2 * at) * wide : (2 * at + 1) * wide] = full
        w_ref[:, (2 * at + 1) * wide : (2 * at + 2) * wide] = full


def prepare(peers, order, lengths, table, damping, radial, one, two):
    modes, nz = damping.shape
    nr = radial.shape[1]
    wide = one.shape[0] * SUB
    return call(
        functools.partial(prep_kernel, peers),
        "prepare",
        (order, lengths, table, damping, radial, one, two),
        [
            shape(modes, nz, nz),
            shape(modes, nz, nz),
            shape(modes, nr, nr),
            shape(modes, nr, nr),
            shape(wide, 4 * wide),
        ],
        8 * modes * nz**3,
        scratch=[pltpu.VMEM((nz, nz), BF), pltpu.VMEM((nz, nz), BF), pltpu.VMEM((nr, nr), BF)],
        smem=2,
    )


def split_kernel(peers, chosen, order_ref, x_ref, *refs):
    outs, sems = refs[:peers], refs[peers]
    block = outs[0].shape[3]
    copies = []
    for k in range(peers):
        start = pl.multiple_of(order_ref[k] * block, block)
        for at, m in enumerate(chosen):
            source = x_ref.at[m, :, :, pl.ds(start, block)]
            copies.append(pltpu.make_async_copy(source, outs[k].at[at], sems.at[k, at]))
    for copy in copies:
        copy.start()
    for copy in copies:
        copy.wait()


def split(peers, order, x, chosen):
    _, comp, rows, nz = x.shape
    number = len(chosen)
    return pl.pallas_call(
        functools.partial(split_kernel, peers, chosen),
        in_specs=[pl.BlockSpec(memory_space=pltpu.SMEM), pl.BlockSpec(memory_space=pltpu.HBM)],
        out_specs=vmem(peers),
        out_shape=[shape(number, comp, rows, nz // peers)] * peers,
        scratch_shapes=[pltpu.SemaphoreType.DMA((peers, number))],
        compiler_params=pltpu.CompilerParams(vmem_limit_bytes=VMEM_LIMIT),
        cost_estimate=pl.CostEstimate(
            flops=0, bytes_accessed=4 * number * comp * rows * nz, transcendentals=0
        ),
        name="split",
    )(order, x)


def by_parity(odd, given, taken):
    @pl.when(odd == 1)
    def _():
        taken[0][...] = given[0][...]
        taken[1][...] = given[1][...]

    @pl.when(odd == 0)
    def _():
        taken[0][...] = given[1][...]
        taken[1][...] = given[0][...]


def assemble_kernel(peers, order_ref, *refs):
    pieces, outs = refs[:peers], refs[peers:]
    rows = pieces[0].shape[2]
    for k in range(peers):
        start = pl.multiple_of(order_ref[peers + k] * rows, rows)
        for at, out in enumerate(outs[:2]):
            out[:, pl.ds(start, rows), :] = pieces[k][at]
    by_parity(order_ref[2 * peers], outs[:2], outs[2:])


def assemble(peers, order, pieces):
    count, comp, rows, block = pieces[0].shape
    return call(
        functools.partial(assemble_kernel, peers),
        "assemble",
        (order, *pieces),
        [shape(comp, rows * peers, block)] * 4,
        0,
        smem=1,
    )


class Chosen:
    def __init__(self, flag, one, other):
        self.flag, self.one, self.other = flag, one, other

    def __getitem__(self, at):
        return jnp.where(self.flag, self.one[at], self.other[at])


def around(own, before, after, m):
    count = len(own)

    def at(i):
        if i < 0:
            return before[-1 - i]
        return own[i] if i < count else after[i - count]

    return [at(m - 1), at(m + 1), at(m - 2), at(m + 2)]


def couple_axial_kernel(peers, modes, count, depth, order_ref, *refs):
    own, refs = refs[:count], refs[count:]
    halos, refs = refs[: 2 * depth], refs[2 * depth :]
    odd = order_ref[2 * peers] == 1
    before = [Chosen(odd, *halos[i : i + 2]) for i in range(0, 2 * depth, 2)]
    after = [Chosen(odd, *halos[i : i + 2][::-1]) for i in range(0, 2 * depth, 2)]
    w_ref, m_ref = refs[:2]
    outs, a_ref = refs[2 : 2 + peers], refs[2 + peers]
    comp, rows, nz = own[0].shape
    wide = comp * SUB
    block = nz // peers
    for at, m in enumerate(modes):
        near = around(own, before, after, m)
        for b in range(rows // SUB):
            part = slice(b * SUB, (b + 1) * SUB)
            field = jnp.concatenate([ref[:, part, :].reshape(wide, nz) for ref in near], axis=0)
            mixed = dot(w_ref[...], field) + own[m][:, part, :].reshape(wide, nz).astype(F32)
            a_ref[b * wide : (b + 1) * wide, :] = mixed.astype(BF)
        result = dot(a_ref[...], m_ref[m]).astype(BF)
        for b in range(rows // SUB):
            for k in range(peers):
                piece = result[b * wide : (b + 1) * wide, k * block : (k + 1) * block]
                outs[k][at, :, b * SUB : (b + 1) * SUB, :] = piece.reshape(comp, SUB, block)


def couple_axial(peers, order, modes, own, halos, weights, matrices):
    count = len(own)
    comp, rows, nz = own[0].shape
    return call(
        functools.partial(couple_axial_kernel, peers, modes, count, len(halos) // 2),
        "couple_axial",
        (order, *own, *halos, weights, matrices),
        [shape(len(modes), comp, rows, nz // peers)] * peers,
        len(modes) * comp * rows * nz * 2 * (nz + 4 * comp * SUB),
        scratch=[pltpu.VMEM((comp * rows, nz), BF)],
        smem=1,
    )


def radial_last_kernel(peers, modes, *refs):
    pieces, r_ref = refs[:peers], refs[peers]
    out_ref, made_ref, sems = refs[-3:]
    comp, _, block = pieces[0].shape[1:]
    copies = []
    for at, m in enumerate(modes):
        for c in range(0, comp, 2):
            field = jnp.concatenate(
                [jnp.concatenate([p[at, c], p[at, c + 1]], axis=1) for p in pieces], axis=0
            )
            result = dot(r_ref[m], field).astype(BF)
            made_ref[at, c] = result[:, :block]
            made_ref[at, c + 1] = result[:, block:]
            copies.append(
                pltpu.make_async_copy(
                    made_ref.at[at, c : c + 2], out_ref.at[m, c : c + 2], sems.at[at, c // 2]
                )
            )
            copies[-1].start()
    for copy in copies:
        copy.wait()


def radial_last(peers, modes, total, pieces, matrices, partial_result):
    count, comp, rows, block = pieces[0].shape
    nr = rows * peers
    specs = vmem(peers + 1)
    args = [*pieces, matrices]
    aliases = {}
    if partial_result is not None:
        specs.append(pl.BlockSpec(memory_space=pltpu.HBM))
        aliases = {len(args): 0}
        args.append(partial_result)
    return pl.pallas_call(
        functools.partial(radial_last_kernel, peers, modes),
        out_shape=shape(total, comp, nr, block),
        in_specs=specs,
        out_specs=pl.BlockSpec(memory_space=pltpu.HBM),
        scratch_shapes=[
            pltpu.VMEM((count, comp, nr, block), BF),
            pltpu.SemaphoreType.DMA((count, comp // 2)),
        ],
        input_output_aliases=aliases,
        compiler_params=pltpu.CompilerParams(vmem_limit_bytes=VMEM_LIMIT),
        cost_estimate=pl.CostEstimate(
            flops=count * comp * nr * nr * block * 2,
            bytes_accessed=count * comp * nr * block * 4,
            transcendentals=0,
        ),
        name="radial_last",
    )(*args)


def couple_radial_kernel(peers, modes, count, depth, order_ref, *refs):
    own, refs = refs[:count], refs[count:]
    halos, refs = refs[: 2 * depth], refs[2 * depth :]
    odd = order_ref[2 * peers] == 1
    before = [Chosen(odd, *halos[i : i + 2]) for i in range(0, 2 * depth, 2)]
    after = [Chosen(odd, *halos[i : i + 2][::-1]) for i in range(0, 2 * depth, 2)]
    w_ref, r_ref = refs[:2]
    outs, a_ref = refs[2 : 2 + peers], refs[2 + peers]
    comp, nr, block = own[0].shape
    rows = nr // peers
    wide = comp * SUB
    for at, m in enumerate(modes):
        near = around(own, before, after, m)

        def side(ref, k):
            parts = [
                ref[:, k * rows + b * SUB : k * rows + (b + 1) * SUB, :].reshape(wide, block)
                for b in range(rows // SUB)
            ]
            return jnp.concatenate(parts, axis=1)

        for k in range(peers):
            field = jnp.concatenate([side(ref, k) for ref in near], axis=0)
            mixed = (dot(w_ref[...], field) + side(own[m], k).astype(F32)).astype(BF)
            for b in range(rows // SUB):
                piece = mixed[:, b * block : (b + 1) * block]
                a_ref[:, k * rows + b * SUB : k * rows + (b + 1) * SUB, :] = piece.reshape(comp, SUB, block)
        for c in range(0, comp, 2):
            field = jnp.concatenate([a_ref[c], a_ref[c + 1]], axis=1)
            result = dot(r_ref[m], field).astype(BF)
            for k in range(peers):
                part = slice(k * rows, (k + 1) * rows)
                outs[k][at, c] = result[part, :block]
                outs[k][at, c + 1] = result[part, block:]


def couple_radial(peers, order, modes, own, halos, weights, matrices):
    comp, nr, block = own[0].shape
    return call(
        functools.partial(couple_radial_kernel, peers, modes, len(own), len(halos) // 2),
        "couple_radial",
        (order, *own, *halos, weights, matrices),
        [shape(len(modes), comp, nr // peers, block)] * peers,
        len(modes) * comp * nr * block * 2 * (4 * comp * SUB + nr),
        scratch=[pltpu.VMEM((comp, nr, block), BF)],
        smem=1,
    )


def axial_kernel(peers, modes, order_ref, *refs):
    pieces, m_ref, outs = refs[:peers], refs[peers], refs[peers + 1 :]
    comp, rows, block = pieces[0].shape[1:]
    for at, m in enumerate(modes):
        field = jnp.concatenate([p[at].reshape(comp * rows, block) for p in pieces], axis=1)
        outs[at][...] = dot(field, m_ref[m]).astype(BF).reshape(comp, rows, peers * block)
    by_parity(order_ref[2 * peers], outs[:2], outs[2:])


def axial(peers, order, modes, pieces, matrices):
    count, comp, rows, block = pieces[0].shape
    nz = block * peers
    return call(
        functools.partial(axial_kernel, peers, modes),
        "axial",
        (order, *pieces, matrices),
        [shape(comp, rows, nz)] * 4,
        count * comp * rows * nz * nz * 2,
        smem=1,
    )


def swap(pieces):
    peers = len(pieces)
    result = list(pieces)
    for k in sorted(range(1, peers), key=lambda k: k == 1):
        result[k] = lax.ppermute(pieces[k], "pencil", [(i, i ^ k) for i in range(peers)])
    return result


RUN = 8


def held(mode, peer):
    turned = (mode // RUN) % 2 * (peer % 2)
    return peer ^ (2 * turned)


def local(cotangent, radial_ops, lengths, couple_one, couple_two, axial_damping):
    peers, ring = lax.axis_size("pencil"), lax.axis_size("mode")
    pairs = ([], [])
    for mode in range(ring):
        beyond = (mode + 1) % ring
        for peer in range(peers):
            one, other = mode * peers + peer, beyond * peers + held(beyond, held(mode, peer))
            pairs[mode % 2].extend([(one, other), (other, one)])
    count = cotangent.shape[0]
    modes = tuple(range(count))

    def exchange(planes):
        return tuple(lax.ppermute(p, ("mode", "pencil"), pair) for p, pair in zip(planes, pairs))

    table = jnp.asarray(cosine_table(axial_damping.shape[1]))
    mode, me = lax.axis_index("mode"), lax.axis_index("pencil")
    others = me ^ jnp.arange(peers, dtype=jnp.int32)
    order = jnp.concatenate([held(mode, others), others, (mode % 2).reshape(1)]).astype(jnp.int32)
    last = count - 1
    inner, outer = (1, last - 1), (0, last)

    cotangent = pltpu.with_memory_space_constraint(cotangent, pltpu.MemorySpace.HBM)
    pieces_outer = swap(split(peers, order, cotangent, outer))
    pieces_inner = split(peers, order, cotangent, inner)
    in_m, out_m, in_r, out_r, weights = prepare(
        peers, order, lengths, table, axial_damping, radial_ops, couple_one, couple_two
    )
    order, weights, pieces_inner, pieces_outer[2] = lax.optimization_barrier(
        (order, weights, pieces_inner, pieces_outer[2])
    )
    pieces_inner = swap(pieces_inner)
    low, high, *sent = assemble(peers, order, pieces_outer)
    near = exchange(sent)
    own = [low, *assemble(peers, order, pieces_inner), high]
    far = exchange(own[3:5])
    own = own[:3] + own[5:]
    pieces_inner = swap(couple_radial(peers, order, inner, own, near, weights, in_r))
    pieces_outer = swap(couple_radial(peers, order, outer, own, near + far, weights, in_r))
    low, high, *far = axial(peers, order, inner, pieces_inner, in_m)
    first, final, *near = axial(peers, order, outer, pieces_outer, in_m)
    near, far = lax.optimization_barrier((near, far))
    near, far = exchange(near), exchange(far)
    own = [first, low, high, final]
    pieces_inner = swap(couple_axial(peers, order, inner, own, near, weights, out_m))
    pieces_outer = swap(couple_axial(peers, order, outer, own, near + far, weights, out_m))
    result = radial_last(peers, inner, count, pieces_inner, out_r, None)
    result = radial_last(peers, outer, count, pieces_outer, out_r, result)
    return result


def solution(mesh):
    return jax.shard_map(
        local,
        mesh=mesh,
        in_specs=(
            P("mode", None, "pencil", None),
            P("mode", None, None),
            P("mode"),
            P(),
            P(),
            P("mode", None),
        ),
        out_specs=P("mode", None, None, "pencil"),
        check_vma=False,
    )
```

```python
import functools
import math

import jax
import jax.numpy as jnp
import numpy as np
from jax import lax
from jax.experimental import pallas as pl
from jax.experimental.pallas import tpu as pltpu
from jax.sharding import PartitionSpec as P

BF = jnp.bfloat16
F32 = jnp.float32
SUB = 16
VMEM_LIMIT = 11 * 1024 * 1024


def cosine_table(count):
    points = np.arange(count, dtype=np.float32)
    scale = np.where(points == 0.0, np.float32(math.sqrt(1.0 / count)), np.float32(math.sqrt(2.0 / count)))
    angle = np.float32(math.pi) * (points[:, None] + np.float32(0.5)) * points[None, :] / np.float32(count)
    return (np.cos(angle).astype(np.float32) * scale[None, :].astype(np.float32)).astype(BF)


def vmem(count):
    return [pl.BlockSpec(memory_space=pltpu.VMEM)] * count


def call(kernel, name, args, outs, flops, scratch=(), smem=0):
    moved = sum(a.size * a.dtype.itemsize for a in args)
    moved += sum(math.prod(o.shape) * o.dtype.itemsize for o in outs)
    return pl.pallas_call(
        kernel,
        out_shape=outs,
        in_specs=[pl.BlockSpec(memory_space=pltpu.SMEM)] * smem + vmem(len(args) - smem),
        out_specs=vmem(len(outs)),
        scratch_shapes=list(scratch),
        compiler_params=pltpu.CompilerParams(vmem_limit_bytes=VMEM_LIMIT),
        cost_estimate=pl.CostEstimate(flops=flops, bytes_accessed=moved, transcendentals=0),
        name=name,
    )(*args)


def dot(a, b):
    return jnp.dot(a, b, preferred_element_type=F32)


def dot_nt(a, b):
    return lax.dot_general(a, b, (((1,), (1,)), ((), ())), preferred_element_type=F32)


def shape(*dims, dtype=BF):
    return jax.ShapeDtypeStruct(dims, dtype)


def prep_kernel(peers, order_ref, len_ref, q_ref, damp_ref, rad_ref, one_ref, two_ref, in_ref, out_ref, rin_ref, rout_ref, w_ref, qh_ref, qp_ref, turned_ref):
    nz = q_ref.shape[0]
    block = nz // peers
    for k in range(peers):
        for at, table in ((k, qh_ref), (peers + k, qp_ref)):
            start = pl.multiple_of(order_ref[at] * block, block)
            table[k * block : (k + 1) * block, :] = q_ref[pl.ds(start, block), :]
    for m in range(damp_ref.shape[0]):
        factor = damp_ref[m : m + 1, :]
        for left, right, out in ((qh_ref, q_ref, in_ref), (q_ref, qp_ref, out_ref)):
            scaled = left[...].astype(F32) * factor
            high = scaled.astype(BF)
            low = (scaled - high.astype(F32)).astype(BF)
            out[m] = (dot_nt(high, right[...]) + dot_nt(low, right[...])).astype(BF)
    nr = rad_ref.shape[1]
    rows = nr // peers
    for m in range(rad_ref.shape[0]):
        index = lax.broadcasted_iota(jnp.int32, (nr, nr), 0)
        turned_ref[...] = jnp.where(index < len_ref[m], rad_ref[m].astype(F32), 0.0).T.astype(BF)
        parts = []
        for k in range(peers):
            start = pl.multiple_of(order_ref[k] * rows, rows)
            rin_ref[m, k * rows : (k + 1) * rows, :] = turned_ref[pl.ds(start, rows), :]
            part = rad_ref[m, pl.ds(start, rows), :].astype(F32)
            index = start + lax.broadcasted_iota(jnp.int32, (rows, nr), 0)
            parts.append(jnp.where(index < len_ref[m], part, 0.0))
        rout_ref[m] = jnp.concatenate(parts, axis=0).T.astype(BF)
    comp = one_ref.shape[0]
    wide = comp * SUB
    row = lax.broadcasted_iota(jnp.int32, (wide, comp), 0) // SUB
    spread = jnp.where(row == lax.broadcasted_iota(jnp.int32, (wide, comp), 1), 1.0, 0.0).astype(BF)
    i = lax.broadcasted_iota(jnp.int32, (wide, wide), 0) % SUB
    j = lax.broadcasted_iota(jnp.int32, (wide, wide), 1) % SUB
    for at, ref in enumerate((one_ref, two_ref)):
        turned = ref[...].astype(BF).astype(F32)
        half = lax.dot_general(spread, turned.astype(BF), (((1,), (1,)), ((), ())), preferred_element_type=F32)
        full = dot_nt(half.astype(BF), spread)
        full = jnp.where(i == j, full, 0.0).astype(BF)
        w_ref[:, (2 * at) * wide : (2 * at + 1) * wide] = full
        w_ref[:, (2 * at + 1) * wide : (2 * at + 2) * wide] = full


def prepare(peers, order, lengths, table, damping, radial, one, two):
    modes, nz = damping.shape
    nr = radial.shape[1]
    wide = one.shape[0] * SUB
    return call(
        functools.partial(prep_kernel, peers),
        "prepare",
        (order, lengths, table, damping, radial, one, two),
        [
            shape(modes, nz, nz),
            shape(modes, nz, nz),
            shape(modes, nr, nr),
            shape(modes, nr, nr),
            shape(wide, 4 * wide),
        ],
        8 * modes * nz**3,
        scratch=[pltpu.VMEM((nz, nz), BF), pltpu.VMEM((nz, nz), BF), pltpu.VMEM((nr, nr), BF)],
        smem=2,
    )


def split_kernel(peers, chosen, order_ref, x_ref, *refs):
    outs, sems = refs[:peers], refs[peers]
    block = outs[0].shape[3]
    copies = []
    for k in range(peers):
        start = pl.multiple_of(order_ref[k] * block, block)
        for at, m in enumerate(chosen):
            source = x_ref.at[m, :, :, pl.ds(start, block)]
            copies.append(pltpu.make_async_copy(source, outs[k].at[at], sems.at[k, at]))
    for copy in copies:
        copy.start()
    for copy in copies:
        copy.wait()


def split(peers, order, x, chosen):
    _, comp, rows, nz = x.shape
    number = len(chosen)
    return pl.pallas_call(
        functools.partial(split_kernel, peers, chosen),
        in_specs=[pl.BlockSpec(memory_space=pltpu.SMEM), pl.BlockSpec(memory_space=pltpu.HBM)],
        out_specs=vmem(peers),
        out_shape=[shape(number, comp, rows, nz // peers)] * peers,
        scratch_shapes=[pltpu.SemaphoreType.DMA((peers, number))],
        compiler_params=pltpu.CompilerParams(vmem_limit_bytes=VMEM_LIMIT),
        cost_estimate=pl.CostEstimate(
            flops=0, bytes_accessed=4 * number * comp * rows * nz, transcendentals=0
        ),
        name="split",
    )(order, x)


def by_parity(odd, given, taken):
    @pl.when(odd == 1)
    def _():
        taken[0][...] = given[0][...]
        taken[1][...] = given[1][...]

    @pl.when(odd == 0)
    def _():
        taken[0][...] = given[1][...]
        taken[1][...] = given[0][...]


def assemble_kernel(peers, order_ref, *refs):
    pieces, outs = refs[:peers], refs[peers:]
    rows = pieces[0].shape[2]
    for k in range(peers):
        start = pl.multiple_of(order_ref[peers + k] * rows, rows)
        for at, out in enumerate(outs[:2]):
            out[:, pl.ds(start, rows), :] = pieces[k][at]
    by_parity(order_ref[2 * peers], outs[:2], outs[2:])


def assemble(peers, order, pieces):
    count, comp, rows, block = pieces[0].shape
    return call(
        functools.partial(assemble_kernel, peers),
        "assemble",
        (order, *pieces),
        [shape(comp, rows * peers, block)] * 4,
        0,
        smem=1,
    )


class Chosen:
    def __init__(self, flag, one, other):
        self.flag, self.one, self.other = flag, one, other

    def __getitem__(self, at):
        return jnp.where(self.flag, self.one[at], self.other[at])


def around(own, before, after, m):
    count = len(own)

    def at(i):
        if i < 0:
            return before[-1 - i]
        return own[i] if i < count else after[i - count]

    return [at(m - 1), at(m + 1), at(m - 2), at(m + 2)]


def couple_axial_kernel(peers, modes, count, depth, order_ref, *refs):
    own, refs = refs[:count], refs[count:]
    halos, refs = refs[: 2 * depth], refs[2 * depth :]
    odd = order_ref[2 * peers] == 1
    before = [Chosen(odd, *halos[i : i + 2]) for i in range(0, 2 * depth, 2)]
    after = [Chosen(odd, *halos[i : i + 2][::-1]) for i in range(0, 2 * depth, 2)]
    w_ref, m_ref = refs[:2]
    outs, a_ref = refs[2 : 2 + peers], refs[2 + peers]
    comp, rows, nz = own[0].shape
    wide = comp * SUB
    block = nz // peers
    for at, m in enumerate(modes):
        near = around(own, before, after, m)
        for b in range(rows // SUB):
            part = slice(b * SUB, (b + 1) * SUB)
            field = jnp.concatenate([ref[:, part, :].reshape(wide, nz) for ref in near], axis=0)
            mixed = dot(w_ref[...], field) + own[m][:, part, :].reshape(wide, nz).astype(F32)
            a_ref[b * wide : (b + 1) * wide, :] = mixed.astype(BF)
        result = dot(a_ref[...], m_ref[m]).astype(BF)
        for b in range(rows // SUB):
            for k in range(peers):
                piece = result[b * wide : (b + 1) * wide, k * block : (k + 1) * block]
                outs[k][at, :, b * SUB : (b + 1) * SUB, :] = piece.reshape(comp, SUB, block)


def couple_axial(peers, order, modes, own, halos, weights, matrices):
    count = len(own)
    comp, rows, nz = own[0].shape
    return call(
        functools.partial(couple_axial_kernel, peers, modes, count, len(halos) // 2),
        "couple_axial",
        (order, *own, *halos, weights, matrices),
        [shape(len(modes), comp, rows, nz // peers)] * peers,
        len(modes) * comp * rows * nz * 2 * (nz + 4 * comp * SUB),
        scratch=[pltpu.VMEM((comp * rows, nz), BF)],
        smem=1,
    )


def radial_last_kernel(peers, modes, *refs):
    pieces, r_ref = refs[:peers], refs[peers]
    out_ref, made_ref, sems = refs[-3:]
    comp, _, block = pieces[0].shape[1:]
    copies = []
    for at, m in enumerate(modes):
        for c in range(0, comp, 2):
            field = jnp.concatenate(
                [jnp.concatenate([p[at, c], p[at, c + 1]], axis=1) for p in pieces], axis=0
            )
            result = dot(r_ref[m], field).astype(BF)
            made_ref[at, c] = result[:, :block]
            made_ref[at, c + 1] = result[:, block:]
            copies.append(
                pltpu.make_async_copy(
                    made_ref.at[at, c : c + 2], out_ref.at[m, c : c + 2], sems.at[at, c // 2]
                )
            )
            copies[-1].start()
    for copy in copies:
        copy.wait()


def radial_last(peers, modes, total, pieces, matrices, partial_result):
    count, comp, rows, block = pieces[0].shape
    nr = rows * peers
    specs = vmem(peers + 1)
    args = [*pieces, matrices]
    aliases = {}
    if partial_result is not None:
        specs.append(pl.BlockSpec(memory_space=pltpu.HBM))
        aliases = {len(args): 0}
        args.append(partial_result)
    return pl.pallas_call(
        functools.partial(radial_last_kernel, peers, modes),
        out_shape=shape(total, comp, nr, block),
        in_specs=specs,
        out_specs=pl.BlockSpec(memory_space=pltpu.HBM),
        scratch_shapes=[
            pltpu.VMEM((count, comp, nr, block), BF),
            pltpu.SemaphoreType.DMA((count, comp // 2)),
        ],
        input_output_aliases=aliases,
        compiler_params=pltpu.CompilerParams(vmem_limit_bytes=VMEM_LIMIT),
        cost_estimate=pl.CostEstimate(
            flops=count * comp * nr * nr * block * 2,
            bytes_accessed=count * comp * nr * block * 4,
            transcendentals=0,
        ),
        name="radial_last",
    )(*args)


def couple_radial_kernel(peers, modes, count, depth, order_ref, *refs):
    own, refs = refs[:count], refs[count:]
    halos, refs = refs[: 2 * depth], refs[2 * depth :]
    odd = order_ref[2 * peers] == 1
    before = [Chosen(odd, *halos[i : i + 2]) for i in range(0, 2 * depth, 2)]
    after = [Chosen(odd, *halos[i : i + 2][::-1]) for i in range(0, 2 * depth, 2)]
    w_ref, r_ref = refs[:2]
    outs, a_ref = refs[2 : 2 + peers], refs[2 + peers]
    comp, nr, block = own[0].shape
    rows = nr // peers
    wide = comp * SUB
    for at, m in enumerate(modes):
        near = around(own, before, after, m)

        def side(ref, k):
            parts = [
                ref[:, k * rows + b * SUB : k * rows + (b + 1) * SUB, :].reshape(wide, block)
                for b in range(rows // SUB)
            ]
            return jnp.concatenate(parts, axis=1)

        for k in range(peers):
            field = jnp.concatenate([side(ref, k) for ref in near], axis=0)
            mixed = (dot(w_ref[...], field) + side(own[m], k).astype(F32)).astype(BF)
            for b in range(rows // SUB):
                piece = mixed[:, b * block : (b + 1) * block]
                a_ref[:, k * rows + b * SUB : k * rows + (b + 1) * SUB, :] = piece.reshape(comp, SUB, block)
        for c in range(0, comp, 2):
            field = jnp.concatenate([a_ref[c], a_ref[c + 1]], axis=1)
            result = dot(r_ref[m], field).astype(BF)
            for k in range(peers):
                part = slice(k * rows, (k + 1) * rows)
                outs[k][at, c] = result[part, :block]
                outs[k][at, c + 1] = result[part, block:]


def couple_radial(peers, order, modes, own, halos, weights, matrices):
    comp, nr, block = own[0].shape
    return call(
        functools.partial(couple_radial_kernel, peers, modes, len(own), len(halos) // 2),
        "couple_radial",
        (order, *own, *halos, weights, matrices),
        [shape(len(modes), comp, nr // peers, block)] * peers,
        len(modes) * comp * nr * block * 2 * (4 * comp * SUB + nr),
        scratch=[pltpu.VMEM((comp, nr, block), BF)],
        smem=1,
    )


def axial_kernel(peers, modes, order_ref, *refs):
    pieces, m_ref, outs = refs[:peers], refs[peers], refs[peers + 1 :]
    comp, rows, block = pieces[0].shape[1:]
    for at, m in enumerate(modes):
        field = jnp.concatenate([p[at].reshape(comp * rows, block) for p in pieces], axis=1)
        outs[at][...] = dot(field, m_ref[m]).astype(BF).reshape(comp, rows, peers * block)
    by_parity(order_ref[2 * peers], outs[:2], outs[2:])


def axial(peers, order, modes, pieces, matrices):
    count, comp, rows, block = pieces[0].shape
    nz = block * peers
    return call(
        functools.partial(axial_kernel, peers, modes),
        "axial",
        (order, *pieces, matrices),
        [shape(comp, rows, nz)] * 4,
        count * comp * rows * nz * nz * 2,
        smem=1,
    )


def swap(pieces):
    peers = len(pieces)
    result = list(pieces)
    for k in sorted(range(1, peers), key=lambda k: k == 1):
        result[k] = lax.ppermute(pieces[k], "pencil", [(i, i ^ k) for i in range(peers)])
    return result


RUN = 8


def held(mode, peer):
    turned = (mode // RUN) % 2 * (peer % 2)
    return peer ^ (2 * turned)


def local(cotangent, radial_ops, lengths, couple_one, couple_two, axial_damping):
    peers, ring = lax.axis_size("pencil"), lax.axis_size("mode")
    pairs = ([], [])
    for mode in range(ring):
        beyond = (mode + 1) % ring
        for peer in range(peers):
            one, other = mode * peers + peer, beyond * peers + held(beyond, held(mode, peer))
            pairs[mode % 2].extend([(one, other), (other, one)])
    count = cotangent.shape[0]
    modes = tuple(range(count))

    def exchange(planes):
        return tuple(lax.ppermute(p, ("mode", "pencil"), pair) for p, pair in zip(planes, pairs))

    table = jnp.asarray(cosine_table(axial_damping.shape[1]))
    mode, me = lax.axis_index("mode"), lax.axis_index("pencil")
    others = me ^ jnp.arange(peers, dtype=jnp.int32)
    order = jnp.concatenate([held(mode, others), others, (mode % 2).reshape(1)]).astype(jnp.int32)
    last = count - 1
    inner, outer = (1, last - 1), (0, last)

    cotangent = pltpu.with_memory_space_constraint(cotangent, pltpu.MemorySpace.HBM)
    pieces_outer = swap(split(peers, order, cotangent, outer))
    pieces_inner = split(peers, order, cotangent, inner)
    in_m, out_m, in_r, out_r, weights = prepare(
        peers, order, lengths, table, axial_damping, radial_ops, couple_one, couple_two
    )
    order, weights, pieces_inner, pieces_outer[2] = lax.optimization_barrier(
        (order, weights, pieces_inner, pieces_outer[2])
    )
    pieces_inner = swap(pieces_inner)
    low, high, *sent = assemble(peers, order, pieces_outer)
    near = exchange(sent)
    own = [low, *assemble(peers, order, pieces_inner), high]
    far = exchange(own[3:5])
    own = own[:3] + own[5:]
    pieces_inner = swap(couple_radial(peers, order, inner, own, near, weights, in_r))
    pieces_outer = swap(couple_radial(peers, order, outer, own, near + far, weights, in_r))
    low, high, *far = axial(peers, order, inner, pieces_inner, in_m)
    first, final, *near = axial(peers, order, outer, pieces_outer, in_m)
    near, far = lax.optimization_barrier((near, far))
    near, far = exchange(near), exchange(far)
    own = [first, low, high, final]
    pieces_inner = swap(couple_axial(peers, order, inner, own, near, weights, out_m))
    pieces_outer = swap(couple_axial(peers, order, outer, own, near + far, weights, out_m))
    result = radial_last(peers, inner, count, pieces_inner, out_r, None)
    result = radial_last(peers, outer, count, pieces_outer, out_r, result)
    return result


def solution(mesh):
    return jax.shard_map(
        local,
        mesh=mesh,
        in_specs=(
            P("mode", None, "pencil", None),
            P("mode", None, None),
            P("mode"),
            P(),
            P(),
            P("mode", None),
        ),
        out_specs=P("mode", None, None, "pencil"),
        check_vma=False,
    )
```
